32 devices in a mesh: ctx: 16 (over z, x, core), head: 2 (over y).
Axes of the slice: x: 2, y: 2, z: 4, core: 2. Of those that a mesh axis runs over, the one named last changes fastest.
Arguments:
- query_proj: bfloat16 [2048, 4096], P('ctx', 'head'), may hold values from -4 to 4
- key_proj: bfloat16 [2048, 4096], P('ctx', 'head'), may hold values from -6 to 6
- value_proj: bfloat16 [2048, 4096], P('ctx', 'head'), may hold values from -6 to 6
- grad_out: bfloat16 [2048, 4096], P('ctx', 'head'), may hold values from -4 to 4
- out_proj: bfloat16 [4096, 4096], P('head'), may hold values from -0.09375 to 0.09375
- filters: bfloat16 [256, 2048], P('head'), may hold values from -1 to 1, as said below
- skip_gain: float32 [4096], P('head'), may hold values from 0.5 to 1.5
- doc_lengths: int32 [4], replicated, may hold values from 1 to 9, 16 in all
- group_of: int32 [4096], P('head'), may hold values from 0 to 255, as said below
Outputs:
- grad_query: bfloat16 [2048, 4096], P('ctx', 'head')
- grad_key: bfloat16 [2048, 4096], P('ctx', 'head')
- grad_filters: float32 [256, 2048], P('head', 'ctx')
The draws below stay inside these ranges and needn't reach their ends.
Inputs may be any that keep to these rules, and one draw needn't show every extreme that they name: `filters`: filter entries never above 1 in magnitude. `group_of`: each filter group is named by exactly 16 channels, and the channels of the k-th block of 2048 channels name only groups k * 128 to (k + 1) * 128 - 1.
All inputs are finite; a program needn't handle non-finite values.
Results may differ from the reference program's by a relative error of at most 0.005.
Values may be sent and summed in bfloat16 or wider, within the bound.
No kernel may reach another device: no remote copies, remote signals or barrier semaphores. Data moves between devices by JAX's collectives and lax.ppermute only.
A program may use at most 128 MiB of HBM per device.

```python
import math
import jax
import jax.numpy as jnp
import numpy as np
from jax import lax

D = 4096
G = 256
TOK_DEV = 128
DOCS = 4
CDEV = 2048
GDEV = 128
CPG = 16
SPANS = 16
L = 2048
N_CTX = 16


def draw_filters(key, part):
    key_rate, key_noise = jax.random.split(key, 2)
    lags = jnp.arange(L, dtype=jnp.float32)
    decay = jnp.exp(jax.random.uniform(key_rate, (G,), jnp.float32, math.log(30.0), math.log(4.0 * L)))
    noise = jnp.clip(jax.random.normal(key_noise, (G, L), jnp.float32), -4.0, 4.0)
    scale = jnp.sqrt(1.0 / jnp.minimum(decay, 1.0 * L))
    values = noise * jnp.exp(-lags[None, :] / decay[:, None]) * scale[:, None]
    return jnp.clip(values, -1.0, 1.0).astype(jnp.bfloat16)


def draw_group_of(key, part):
    shards = D // CDEV
    keys = jax.random.split(jax.random.fold_in(key, 7), shards)
    perms = jax.vmap(lambda single: jax.random.permutation(single, CDEV))(keys)
    base = jnp.arange(shards, dtype=jnp.int32)[:, None] * GDEV
    return (base + perms.astype(jnp.int32) // CPG).reshape(D).astype(jnp.int32)


def shard_levels(rng, shape, cuts, smallest, high):
    gain = 1.0
    for position, shards_of in cuts:
        heights = jax.random.uniform(jax.random.fold_in(jax.random.fold_in(rng, 6), position), (shards_of,), jnp.float32, smallest / len(cuts), high / len(cuts))
        gain = gain * jnp.repeat(jnp.exp(heights), shape[position] // shards_of).reshape((-1,) + (1,) * (len(shape) - 1 - position))
    return gain


def split_up(amount, total, limit, lean):
    loads = [(1 << 20) // math.isqrt(rank ** lean) + 1 for rank in range(2, amount + 1)]
    rest, holding = total - limit - (amount - 1), [1] * (amount - 1)
    while rest > 0:
        free = [i for i in range(amount - 1) if holding[i] < limit]
        pool, remaining = sum([loads[i] for i in free]), rest
        for i in free:
            more = min(limit - holding[i], max(1, remaining * loads[i] // pool), rest)
            holding[i] = holding[i] + more
            rest = rest - more
    return np.array([limit] + holding)


def uneven(rng, amount, total, bound, skew):
    if amount == 2:
        one = jax.random.randint(rng, (), max(1, total - bound), min(bound, total - 1) + 1)
        return jnp.stack([one, total - one])
    lengths = jnp.asarray(split_up(amount, total, bound, skew), jnp.int32)
    twos = (amount - 1) // 2
    donor, receiver = lengths[1:1 + 2 * twos:2], lengths[2:2 + 2 * twos:2]
    slack = jnp.minimum(donor - 1, bound - receiver)
    shifted = jax.random.randint(jax.random.fold_in(rng, 1), (twos,), 0, 1 << 20) % (slack + 1)
    lengths = lengths.at[1:1 + 2 * twos:2].set(donor - shifted).at[2:2 + 2 * twos:2].set(receiver + shifted)
    return lengths[jax.random.permutation(jax.random.fold_in(rng, 2), amount)]


def bell_draw(own_key, dims, width, bound, cuts=(), kind=jnp.bfloat16):
    array = width * jax.random.normal(own_key, dims, jnp.float32)
    if cuts:
        array = array * shard_levels(own_key, dims, cuts, -0.22, 0.18)
    return jnp.clip(array, -bound, bound).astype(kind)


def setup_inputs(seed: int = 0) -> dict:
    splits = jax.random.split(jax.random.key(seed), 10)
    return {
        "query_proj": bell_draw(splits[0], (L, D), 0.25, 4.0, ((0, 16), (1, 2))),
        "key_proj": bell_draw(splits[1], (L, D), 1.0, 6.0, ((0, 16), (1, 2))),
        "value_proj": bell_draw(splits[2], (L, D), 1.0, 6.0, ((0, 16), (1, 2))),
        "grad_out": bell_draw(splits[3], (L, D), 0.25, 4.0, ((0, 16), (1, 2))),
        "out_proj": bell_draw(splits[4], (D, D), D ** -0.5, 0.09375, ((0, 2),)),
        "filters": draw_filters(jax.random.fold_in(splits[9], 71), 0),
        "skip_gain": jnp.clip(0.5 + 1.0 * jax.random.uniform(splits[6], (D,), jnp.float32) ** shard_levels(splits[6], (D,), ((0, 2),), -0.2, 0.2), 0.5, 1.5),
        "doc_lengths": uneven(splits[7], DOCS, SPANS, SPANS // 2 + 1, 0).astype(jnp.int32),
        "group_of": draw_group_of(jax.random.fold_in(splits[9], 71), 0),
    }


def reference(query_proj, key_proj, value_proj, grad_out, out_proj, filters, skip_gain, doc_lengths, group_of):
    length = TOK_DEV * N_CTX
    feature_grad = jnp.dot(grad_out, out_proj.T, preferred_element_type=jnp.float32)
    conv_grad = (feature_grad * value_proj.astype(jnp.float32)).astype(jnp.bfloat16)
    gated = (query_proj.astype(jnp.float32) * key_proj.astype(jnp.float32)).astype(jnp.bfloat16)
    conv_grad, gated = lax.optimization_barrier((conv_grad, gated))
    conv_grad = conv_grad.astype(jnp.float32)
    gated = gated.astype(jnp.float32)
    span_index = (jnp.arange(length) // TOK_DEV).astype(jnp.int32)
    bounds = jnp.cumsum(doc_lengths).astype(jnp.int32)
    token_doc = jnp.sum((bounds[None, :] <= span_index[:, None]).astype(jnp.int32), axis=1)
    doc_masks = (token_doc[None, :] == jnp.arange(DOCS, dtype=jnp.int32)[:, None]).astype(jnp.float32)
    filt = filters.astype(jnp.float32)
    block_cols = min(256, D)
    blocks = D // block_cols
    stacked = (conv_grad.T.reshape(blocks, block_cols, length), gated.T.reshape(blocks, block_cols, length),
               query_proj.astype(jnp.float32).T.reshape(blocks, block_cols, length),
               key_proj.astype(jnp.float32).T.reshape(blocks, block_cols, length),
               group_of.reshape(blocks, block_cols), skip_gain.reshape(blocks, block_cols))

    def one_block(filter_grad, entry):
        grad_rows, gate_rows, query_rows, key_rows, group_rows, skip_rows = entry
        channel_filt = jnp.take(filt, group_rows, axis=0)
        filt_spec = jnp.fft.rfft(channel_filt, n=2 * length)
        gated_grad = jnp.zeros((block_cols, length), jnp.float32)
        lag_sums = jnp.zeros((block_cols, length), jnp.float32)
        for doc_index in range(DOCS):
            grad_doc = grad_rows * doc_masks[doc_index]
            gate_doc = gate_rows * doc_masks[doc_index]
            grad_spec = jnp.fft.rfft(grad_doc, n=2 * length)
            back = jnp.fft.irfft(grad_spec * jnp.conj(filt_spec), n=2 * length)[:, :length]
            gated_grad = gated_grad + back.astype(jnp.float32) * doc_masks[doc_index]
            corr = jnp.fft.irfft(grad_spec * jnp.conj(jnp.fft.rfft(gate_doc, n=2 * length)), n=2 * length)[:, :length]
            lag_sums = lag_sums + corr.astype(jnp.float32)
        gated_grad = gated_grad + skip_rows[:, None] * grad_rows
        query_out = (gated_grad * key_rows).astype(jnp.bfloat16)
        key_out = (gated_grad * query_rows).astype(jnp.bfloat16)
        onehot = (group_rows[None, :] == jnp.arange(G, dtype=jnp.int32)[:, None]).astype(jnp.float32)
        filter_grad = filter_grad + jnp.dot(onehot, lag_sums, precision=lax.Precision.HIGHEST)
        return filter_grad, (query_out, key_out)

    grad_filters, outs = lax.scan(one_block, jnp.zeros((G, length), jnp.float32), stacked)
    grad_query = outs[0].reshape(D, length).T
    grad_key = outs[1].reshape(D, length).T
    return grad_query, grad_key, grad_filters
```

```python
import functools

import jax
import jax.numpy as jnp
from jax import lax
from jax.experimental import pallas as pl
from jax.experimental.pallas import tpu as pltpu
from jax.sharding import PartitionSpec as P

F32 = jnp.float32
BF16 = jnp.bfloat16
I32 = jnp.int32
NT = (((1,), (1,)), ((), ()))
NN = (((1,), (0,)), ((), ()))
EXTRA = 16


def dot(a, b, dims):
    return lax.dot_general(a, b, dims, preferred_element_type=F32)


def one_hot(rank_row, first, rows):
    shape = (rows, rank_row.shape[1])
    return jnp.where(lax.broadcasted_iota(I32, shape, 0) + first == rank_row, 1.0, 0.0).astype(BF16)


def params(**kw):
    return pltpu.CompilerParams(vmem_limit_bytes=56 * 1024 * 1024, **kw)


def gate_kernel(head_ref, group_ref, query_ref, key_ref, out_ref, rank_ref, *, groups, per_group, chunk):
    channels = group_ref.shape[1]
    local = group_ref[...] - head_ref[0] * groups
    width = 128
    upper = (
        lax.broadcasted_iota(I32, (width, width), 0) < lax.broadcasted_iota(I32, (width, width), 1)
    )
    upper = jnp.where(upper, 1.0, 0.0).astype(BF16)
    base = jnp.zeros((groups, 1), F32)
    for b in range(channels // width):
        here = local[:, b * width : (b + 1) * width]
        member = jnp.where(lax.broadcasted_iota(I32, (groups, width), 0) == here, 1.0, 0.0)
        before = dot(member.astype(BF16), upper, NN) + base
        place = jnp.sum(member * before, axis=0, keepdims=True)
        rank_ref[:, b * width : (b + 1) * width] = here * per_group + place.astype(I32)
        base = base + jnp.sum(member, axis=1, keepdims=True)
    rank = rank_ref[...]
    gated = (query_ref[...].astype(F32) * key_ref[...].astype(F32)).astype(BF16)
    gated_t = gated.T
    permute_rows(rank, gated_t, out_ref, chunk)


def permute_rows(rank, by_channel, out_ref, chunk):
    channels = by_channel.shape[0]
    rows = out_ref.shape[1]
    for p in range(0, channels, chunk):
        moved = dot(one_hot(rank, p, chunk), by_channel, NN).astype(BF16)
        out_ref[p // rows : (p + chunk) // rows] = moved.reshape(chunk // rows, rows, -1)


def partial_kernel(half_ref, grad_ref, weight_ref, out_ref):
    out_ref[...] = dot(weight_ref[...], grad_ref[...], NT)


def add_kernel(half_ref, grad_ref, weight_ref, acc_ref, out_ref):
    out_ref[...] = acc_ref[...] + dot(weight_ref[...], grad_ref[...], NT)


def last_kernel(
    half_ref, rank_ref, grad_ref, weight_ref, acc_ref, value_ref, out_ref, conv_ref, *, chunk
):
    step = pl.program_id(0)
    block = weight_ref.shape[0]
    total = acc_ref[...] + dot(weight_ref[...], grad_ref[...], NT)
    conv = (total * value_ref[...].astype(F32).T).astype(BF16)
    conv_ref[pl.ds(pl.multiple_of(step * block, block), block), :] = conv

    @pl.when(step == pl.num_programs(0) - 1)
    def _():
        permute_rows(rank_ref[...], conv_ref[...], out_ref, chunk)


def prepare_kernel(docs_ref, filt_ref, toep_ref, mask_ref, *, per_group, spans):
    groups, width = filt_ref.shape
    tokens = toep_ref.shape[1]
    for g in range(groups):
        row = jnp.concatenate([filt_ref[g : g + 1, :], jnp.zeros((1, tokens), F32)], axis=1)
        wide = jnp.broadcast_to(row, (tokens, width + tokens))
        skewed = pltpu.roll(wide, 0, 1, stride=1, stride_axis=0)
        toep_ref[g] = skewed[:, :width].astype(BF16)
    rows = mask_ref.shape[0]
    block = lax.broadcasted_iota(I32, (rows, tokens), 0) // per_group

    def doc_of(index):
        bound = 0
        doc = jnp.zeros(index.shape, I32)
        for d in range(docs_ref.shape[0]):
            bound = bound + docs_ref[d]
            doc = doc + jnp.where(index >= bound, 1, 0)
        return doc

    mine = doc_of(block)
    for k in range(width // tokens):
        same = (doc_of(block + k) == mine) & (block + k < spans)
        mask_ref[:, k * tokens : (k + 1) * tokens] = jnp.where(same, 1.0, 0.0).astype(BF16)


def conv_kernel(grad_ref, gate_ref, toep_ref, mask_ref, out_ref, moved_ref, sums_ref, *, per_group):
    step = pl.program_id(0)
    spans, rows, tokens = grad_ref.shape
    here = rows // per_group
    lags = mask_ref.shape[1]
    reach = lags // tokens
    channels = out_ref.shape[1] - EXTRA

    @pl.when(step == 0)
    def _():
        moved_ref[...] = jnp.zeros(moved_ref.shape, BF16)
        sums_ref[...] = jnp.zeros(sums_ref.shape, F32)

    flip = lax.broadcasted_iota(I32, (tokens, tokens), 0) + lax.broadcasted_iota(I32, (tokens, tokens), 1)
    flip = jnp.where(flip == tokens - 1, 1.0, 0.0).astype(BF16)
    for g in range(here):
        grad = grad_ref[:, g * per_group : (g + 1) * per_group, :].reshape(spans * per_group, tokens)
        for k in range(reach):
            keep = (spans - k) * per_group
            cols = slice(k * tokens, (k + 1) * tokens)
            moved_ref[g, :keep, cols] = grad[k * per_group :, :] * mask_ref[:keep, cols]
        moved = moved_ref[g]
        back = dot(moved, toep_ref[g], NT)
        start = pl.multiple_of((step * here + g) * per_group, per_group)
        out_ref[:, pl.ds(start, per_group), :] = back.astype(BF16).reshape(spans, per_group, tokens)
        gate = gate_ref[:, g * per_group : (g + 1) * per_group, :].reshape(spans * per_group, tokens)
        gate_t = dot(flip, gate, NT).astype(BF16)
        corr = dot(gate_t, moved, NN)
        wide = jnp.concatenate([corr, jnp.zeros((tokens, tokens), F32)], axis=1)
        skewed = pltpu.roll(wide, lags + 1, 1, stride=1, stride_axis=0)
        sums_ref[pl.ds(step * here + g, 1), :] = jnp.sum(skewed[:, :lags], axis=0, keepdims=True)

    @pl.when(step == pl.num_programs(0) - 1)
    def _():
        for k in range(spans):
            if k < reach:
                exact = sums_ref[:, k * tokens : (k + 1) * tokens]
                high = exact.astype(BF16).astype(F32)
                both = jnp.concatenate([high, exact - high], axis=0).astype(BF16)
            else:
                both = jnp.zeros((EXTRA, tokens), BF16)
            out_ref[k, channels:, :] = both


def skip_kernel(conv_ref, skip_ref, out_ref):
    out_ref[...] = conv_ref[...].astype(F32).T * skip_ref[...]


def gates_kernel(
    back_ref, rank_ref, skip_ref, query_ref, key_ref, grad_query_ref, grad_key_ref, filt_ref, sorted_ref, *, sub_groups
):
    spans, rows, tokens = back_ref.shape
    sub = rows - EXTRA

    @pl.when(pl.program_id(0) == 0)
    def _():
        flat = back_ref[:, :sub, :].reshape(spans * sub, tokens)
        sorted_ref[...] = flat.T
        for d in range(spans):
            tail = back_ref[d, sub:, :].astype(F32)
            both = tail[: EXTRA // 2] + tail[EXTRA // 2 :]
            filt_ref[d * sub_groups : (d + 1) * sub_groups, :] = both[:sub_groups]

    channels = sorted_ref.shape[1]
    conv = dot(sorted_ref[...], one_hot(rank_ref[...], 0, channels), NN)
    gated_grad = conv + skip_ref[...]
    grad_query_ref[...] = (gated_grad * key_ref[...].astype(F32)).astype(BF16)
    grad_key_ref[...] = (gated_grad * query_ref[...].astype(F32)).astype(BF16)


def whole(shape):
    return pl.BlockSpec(shape, lambda *_: (0,) * len(shape))


def scalars():
    return pl.BlockSpec(memory_space=pltpu.SMEM)


def per_device(
    query_proj, key_proj, value_proj, grad_out, out_proj, filters, skip_gain, doc_lengths, group_of
):
    tokens, channels = query_proj.shape
    groups = filters.shape[0]
    per_group = channels // groups
    spans = lax.axis_size("ctx")
    heads = lax.axis_size("head")
    position = lax.axis_index("ctx")
    head = lax.axis_index("head")
    sub = channels // spans
    sub_groups = sub // per_group
    reach = spans // 2 + 1
    lags = reach * tokens
    chunk = min(256, channels)

    arrived = [
        lax.ppermute(grad_out, "head", [(i, (i + r) % heads) for i in range(heads)])
        for r in range(1, heads)
    ]

    gate_sorted, rank = pl.pallas_call(
        functools.partial(gate_kernel, groups=groups, per_group=per_group, chunk=chunk),
        out_shape=(
            jax.ShapeDtypeStruct((spans, sub, tokens), BF16),
            jax.ShapeDtypeStruct((1, channels), I32),
        ),
        in_specs=[scalars(), whole((1, channels)), whole((tokens, channels)), whole((tokens, channels))],
        out_specs=(whole((spans, sub, tokens)), whole((1, channels))),
        compiler_params=params(),
        name="gate",
    )(head.reshape(1), group_of.reshape(1, channels), query_proj, key_proj)
    gate_moved = lax.all_to_all(gate_sorted, "ctx", 0, 0)

    block = min(256, channels)
    feats = grad_out.shape[1]
    steps = channels // block
    acc = None
    for r, grad in enumerate([grad_out] + arrived):
        source = ((head + heads - r) % heads).reshape(1)
        grad_spec = pl.BlockSpec((tokens, feats), lambda j, s: (0, 0))
        weight_spec = pl.BlockSpec((block, feats), lambda j, s: (j, s[0]))
        acc_spec = pl.BlockSpec((block, tokens), lambda j, s: (j, 0))
        if r < heads - 1:
            first = acc is None
            acc = pl.pallas_call(
                partial_kernel if first else add_kernel,
                out_shape=jax.ShapeDtypeStruct((channels, tokens), F32),
                grid_spec=pltpu.PrefetchScalarGridSpec(
                    num_scalar_prefetch=1,
                    grid=(steps,),
                    in_specs=[grad_spec, weight_spec] + ([] if first else [acc_spec]),
                    out_specs=acc_spec,
                ),
                compiler_params=params(),
                name="own" if first else "more",
            )(source, grad, out_proj, *([] if first else [acc]))
        else:
            conv_sorted, conv_grad = pl.pallas_call(
                functools.partial(last_kernel, chunk=chunk),
                out_shape=(
                    jax.ShapeDtypeStruct((spans, sub, tokens), BF16),
                    jax.ShapeDtypeStruct((channels, tokens), BF16),
                ),
                grid_spec=pltpu.PrefetchScalarGridSpec(
                    num_scalar_prefetch=1,
                    grid=(steps,),
                    in_specs=[
                        pl.BlockSpec((1, channels), lambda j, s: (0, 0)),
                        grad_spec,
                        weight_spec,
                        acc_spec,
                        pl.BlockSpec((tokens, block), lambda j, s: (0, j)),
                    ],
                    out_specs=(
                        pl.BlockSpec((spans, sub, tokens), lambda j, s: (0, 0, 0)),
                        pl.BlockSpec((channels, tokens), lambda j, s: (0, 0)),
                    ),
                ),
                compiler_params=params(),
                name="last",
            )(source, rank, grad, out_proj, acc, value_proj)
    conv_moved = lax.all_to_all(conv_sorted, "ctx", 0, 0)

    filt_sub = lax.dynamic_slice(filters, (position * sub_groups, 0), (sub_groups, lags)).astype(F32)
    toep, mask = pl.pallas_call(
        functools.partial(prepare_kernel, per_group=per_group, spans=spans),
        out_shape=(
            jax.ShapeDtypeStruct((sub_groups, tokens, lags), BF16),
            jax.ShapeDtypeStruct((spans * per_group, lags), BF16),
        ),
        in_specs=[scalars(), whole((sub_groups, lags))],
        out_specs=(whole((sub_groups, tokens, lags)), whole((spans * per_group, lags))),
        compiler_params=params(),
        name="prepare",
    )(doc_lengths, filt_sub)
    skip_part = pl.pallas_call(
        skip_kernel,
        out_shape=jax.ShapeDtypeStruct((tokens, channels), F32),
        in_specs=[whole((channels, tokens)), whole((1, channels))],
        out_specs=whole((tokens, channels)),
        compiler_params=params(),
        name="skip",
    )(conv_grad, skip_gain.reshape(1, channels))

    here = 2 if sub_groups % 2 == 0 else 1
    back = pl.pallas_call(
        functools.partial(conv_kernel, per_group=per_group),
        out_shape=jax.ShapeDtypeStruct((spans, sub + EXTRA, tokens), BF16),
        grid=(sub_groups // here,),
        in_specs=[
            pl.BlockSpec((spans, here * per_group, tokens), lambda g: (0, g, 0)),
            pl.BlockSpec((spans, here * per_group, tokens), lambda g: (0, g, 0)),
            pl.BlockSpec((here, tokens, lags), lambda g: (g, 0, 0)),
            whole((spans * per_group, lags)),
        ],
        out_specs=whole((spans, sub + EXTRA, tokens)),
        scratch_shapes=[
            pltpu.VMEM((here, spans * per_group, lags), BF16),
            pltpu.VMEM((EXTRA // 2, lags), F32),
        ],
        compiler_params=params(),
        name="conv",
    )(conv_moved, gate_moved, toep, mask)
    back_moved = lax.all_to_all(back, "ctx", 0, 0)

    cols = pl.BlockSpec((tokens, block), lambda j: (0, j))
    grad_query, grad_key, grad_filters = pl.pallas_call(
        functools.partial(gates_kernel, sub_groups=sub_groups),
        out_shape=(
            jax.ShapeDtypeStruct((tokens, channels), BF16),
            jax.ShapeDtypeStruct((tokens, channels), BF16),
            jax.ShapeDtypeStruct((groups, tokens), F32),
        ),
        grid=(steps,),
        in_specs=[
            whole((spans, sub + EXTRA, tokens)),
            pl.BlockSpec((1, block), lambda j: (0, j)),
            cols,
            cols,
            cols,
        ],
        out_specs=(cols, cols, whole((groups, tokens))),
        scratch_shapes=[pltpu.VMEM((tokens, channels), BF16)],
        compiler_params=params(),
        name="gates",
    )(back_moved, rank, skip_part, query_proj, key_proj)
    return (grad_query, grad_key, grad_filters)


def solution(mesh):
    in_specs = (
        P("ctx", "head"),
        P("ctx", "head"),
        P("ctx", "head"),
        P("ctx", "head"),
        P("head", None),
        P("head", None),
        P("head"),
        P(),
        P("head"),
    )
    out_specs = (P("ctx", "head"), P("ctx", "head"), P("head", "ctx"))
    return jax.shard_map(
        per_device, mesh=mesh, in_specs=in_specs, out_specs=out_specs, check_vma=False
    )
```

```python
import functools

import jax
import jax.numpy as jnp
from jax import lax
from jax.experimental import pallas as pl
from jax.experimental.pallas import tpu as pltpu
from jax.sharding import PartitionSpec as P

F32 = jnp.float32
BF16 = jnp.bfloat16
I32 = jnp.int32
NT = (((1,), (1,)), ((), ()))
NN = (((1,), (0,)), ((), ()))
LANES = 128
EXTRA = 16
VMEM = pl.BlockSpec(memory_space=pltpu.VMEM)
SMEM = pl.BlockSpec(memory_space=pltpu.SMEM)
ANY = pl.BlockSpec(memory_space=pl.ANY)


def dot(a, b, dims):
    return lax.dot_general(a, b, dims, preferred_element_type=F32)


def on_chip(x):
    return pltpu.with_memory_space_constraint(x, pltpu.VMEM)


def call(kernel, out_shape, in_specs, scratch=(), out_specs=None):
    return pl.pallas_call(
        kernel,
        out_shape=out_shape,
        in_specs=in_specs,
        out_specs=jax.tree.map(lambda _: VMEM, out_shape) if out_specs is None else out_specs,
        scratch_shapes=scratch,
        compiler_params=pltpu.CompilerParams(vmem_limit_bytes=56 * 1024 * 1024),
    )


def rank_column(rank_row, column_ref):
    wide = jnp.broadcast_to(rank_row.astype(F32), (LANES, rank_row.shape[1]))
    column_ref[...] = wide.T.astype(I32)


def permute(by_token, column_ref, out_ref):
    channels = column_ref.shape[0]
    rows = out_ref.shape[1]
    width = min(2 * LANES, channels)
    lane = lax.broadcasted_iota(I32, (channels, LANES), 1)
    for p in range(0, channels, width):
        picks = [
            jnp.where(column_ref[...] == lane + (p + q), 1.0, 0.0).astype(BF16)
            for q in range(0, width, LANES)
        ]
        moved = dot(by_token, jnp.concatenate(picks, axis=1), NN).T.astype(BF16)
        out_ref[p // rows : (p + width) // rows] = moved.reshape(width // rows, rows, -1)


def gate_kernel(
    head_ref, group_ref, query_hbm, key_hbm, out_ref, rank_ref, query_ref, key_ref, column_ref, sem, *, groups, per_group
):
    loads = [
        pltpu.make_async_copy(query_hbm, query_ref, sem.at[0]),
        pltpu.make_async_copy(key_hbm, key_ref, sem.at[1]),
    ]
    for load in loads:
        load.start()
    channels = group_ref.shape[1]
    local = group_ref[...] - head_ref[0] * groups
    upper = lax.broadcasted_iota(I32, (LANES, LANES), 0) < lax.broadcasted_iota(I32, (LANES, LANES), 1)
    upper = jnp.where(upper, 1.0, 0.0).astype(BF16)
    base = jnp.zeros((groups, 1), F32)
    for b in range(channels // LANES):
        here = local[:, b * LANES : (b + 1) * LANES]
        member = jnp.where(lax.broadcasted_iota(I32, (groups, LANES), 0) == here, 1.0, 0.0)
        before = dot(member.astype(BF16), upper, NN) + base
        place = jnp.sum(member * before, axis=0, keepdims=True)
        rank_ref[:, b * LANES : (b + 1) * LANES] = here * per_group + place.astype(I32)
        base = base + jnp.sum(member, axis=1, keepdims=True)
    rank_column(rank_ref[...], column_ref)
    for load in loads:
        load.wait()
    gated = (query_ref[...].astype(F32) * key_ref[...].astype(F32)).astype(BF16)
    permute(gated, column_ref, out_ref)


def stream_weights(half, weight_hbm, weight_ref, sem):
    _, feats = weight_ref.shape
    count = sem.shape[0]
    width = feats // count
    copies = [
        pltpu.make_async_copy(
            weight_hbm.at[:, pl.ds(pl.multiple_of(half * feats + j * width, width), width)],
            weight_ref.at[:, pl.ds(j * width, width)],
            sem.at[j],
        )
        for j in range(count)
    ]
    for copy in copies:
        copy.start()
    return copies, width


def product(copies, width, grad_ref, weight_ref, out_ref, fresh):
    for j, copy in enumerate(copies):
        copy.wait()
        cols = slice(j * width, (j + 1) * width)
        part = dot(grad_ref[:, cols], weight_ref[:, cols], NT)
        out_ref[...] = part if fresh and j == 0 else out_ref[...] + part


def partial_kernel(half_ref, grad_hbm, weight_hbm, *refs):
    *acc, out_ref, grad_ref, weight_ref, sem, grad_sem = refs
    load = pltpu.make_async_copy(grad_hbm, grad_ref, grad_sem)
    load.start()
    copies, width = stream_weights(half_ref[0], weight_hbm, weight_ref, sem)
    if acc:
        out_ref[...] = acc[0][...]
    load.wait()
    product(copies, width, grad_ref, weight_ref, out_ref, not acc)


def last_kernel(
    half_ref, rank_ref, grad_ref, acc_ref, weight_hbm, value_hbm, out_ref, conv_ref, total_ref, weight_ref, value_ref, column_ref, sem, value_sem
):
    load = pltpu.make_async_copy(value_hbm, value_ref, value_sem)
    copies, width = stream_weights(half_ref[0], weight_hbm, weight_ref, sem)
    load.start()
    rank_column(rank_ref[...], column_ref)
    total_ref[...] = acc_ref[...]
    product(copies, width, grad_ref, weight_ref, total_ref, False)
    load.wait()
    conv_ref[...] = (total_ref[...] * value_ref[...].astype(F32)).astype(BF16)
    permute(conv_ref[...], column_ref, out_ref)


def prepare_kernel(docs_ref, filt_ref, gate_ref, skip_ref, gate_t_ref, rows_ref, doc_ref, skip_out_ref, *, per_group):
    spans, _, tokens = gate_ref.shape
    groups, lags = filt_ref.shape
    flip = lax.broadcasted_iota(I32, (tokens, tokens), 0) + lax.broadcasted_iota(I32, (tokens, tokens), 1)
    flip = jnp.where(flip == tokens - 1, 1.0, 0.0).astype(BF16)
    for g in range(groups):
        gate = gate_ref[:, g * per_group : (g + 1) * per_group, :].reshape(spans * per_group, tokens)
        gate_t_ref[g] = dot(flip, gate, NT).astype(BF16)
    rows_ref[:, :lags] = filt_ref[...]
    rows_ref[:, lags:] = jnp.zeros((groups, tokens), F32)
    index = lax.broadcasted_iota(I32, doc_ref.shape, 0) // per_group
    bound = 0
    doc = jnp.zeros(doc_ref.shape, F32)
    for d in range(docs_ref.shape[0]):
        bound = bound + docs_ref[d]
        doc = doc + jnp.where(index >= bound, 1.0, 0.0)
    doc_ref[...] = doc
    skip_out_ref[...] = skip_ref[...]


def conv_kernel(grad_ref, gate_t_ref, rows_ref, doc_ref, out_ref, moved_ref, sums_ref, *, per_group):
    spans, sub, tokens = grad_ref.shape
    groups, padded = rows_ref.shape
    lags = padded - tokens
    reach = lags // tokens
    for k in range(reach):
        cut = k * per_group
        keep = (spans - k) * per_group
        same = jnp.where(doc_ref[cut:, :] == doc_ref[:keep, :], 1.0, 0.0).astype(BF16)
        cols = slice(k * tokens, (k + 1) * tokens)
        for g in range(groups):
            grad = grad_ref[k:, g * per_group : (g + 1) * per_group, :].reshape(keep, tokens)
            moved_ref[g, :keep, cols] = grad * same
            if k:
                moved_ref[g, keep:, cols] = jnp.zeros((cut, tokens), BF16)
    sums_ref[...] = jnp.zeros(sums_ref.shape, F32)
    for g in range(groups):
        moved = moved_ref[g]
        wide = jnp.broadcast_to(rows_ref[g : g + 1, :], (tokens, padded))
        toeplitz = pltpu.roll(wide, 0, 1, stride=1, stride_axis=0)[:, :lags].astype(BF16)
        back = dot(moved, toeplitz, NT)
        out_ref[:, g * per_group : (g + 1) * per_group, :] = back.astype(BF16).reshape(spans, per_group, tokens)
        corr = dot(gate_t_ref[g], moved, NN)
        wide = jnp.concatenate([corr, jnp.zeros((tokens, tokens), F32)], axis=1)
        skewed = pltpu.roll(wide, lags + 1, 1, stride=1, stride_axis=0)
        sums_ref[g : g + 1, :] = jnp.sum(skewed[:, :lags], axis=0, keepdims=True)
    for k in range(spans):
        if k < reach:
            exact = sums_ref[:, k * tokens : (k + 1) * tokens]
            high = exact.astype(BF16).astype(F32)
            both = jnp.concatenate([high, exact - high], axis=0).astype(BF16)
        else:
            both = jnp.zeros((EXTRA, tokens), BF16)
        out_ref[k, sub:, :] = both


def gates_kernel(
    back_ref, rank_ref, conv_ref, skip_ref, query_hbm, key_hbm, grad_query_hbm, grad_key_hbm, filt_hbm,
    query_ref, key_ref, grad_query_ref, grad_key_ref, filt_ref, sorted_ref, load_sem, store_sem, filt_sem, *, sub_groups
):
    spans, rows, tokens = back_ref.shape
    sub = rows - EXTRA
    channels = rank_ref.shape[1]
    loads = [
        pltpu.make_async_copy(query_hbm, query_ref, load_sem.at[0]),
        pltpu.make_async_copy(key_hbm, key_ref, load_sem.at[1]),
    ]
    for load in loads:
        load.start()
    for d in range(spans):
        tail = back_ref[d, sub:, :].astype(F32)
        both = tail[: EXTRA // 2] + tail[EXTRA // 2 :]
        filt_ref[d * sub_groups : (d + 1) * sub_groups, :] = both[:sub_groups]
    stores = [pltpu.make_async_copy(filt_ref, filt_hbm, filt_sem)]
    stores[0].start()
    sorted_ref[...] = back_ref[:, :sub, :].reshape(spans * sub, tokens).T
    for load in loads:
        load.wait()
    width = channels // store_sem.shape[1]
    for j in range(store_sem.shape[1]):
        cols = slice(j * width, (j + 1) * width)
        place = lax.broadcasted_iota(I32, (channels, width), 0)
        picks = jnp.where(place == rank_ref[:, cols], 1.0, 0.0).astype(BF16)
        gated_grad = dot(sorted_ref[...], picks, NN) + conv_ref[:, cols].astype(F32) * skip_ref[:, cols]
        grad_query_ref[:, cols] = (gated_grad * key_ref[:, cols].astype(F32)).astype(BF16)
        grad_key_ref[:, cols] = (gated_grad * query_ref[:, cols].astype(F32)).astype(BF16)
        for which, (source, target) in enumerate(((grad_query_ref, grad_query_hbm), (grad_key_ref, grad_key_hbm))):
            part = pl.ds(j * width, width)
            stores.append(pltpu.make_async_copy(source.at[:, part], target.at[:, part], store_sem.at[which, j]))
            stores[-1].start()
    for store in stores:
        store.wait()


def per_device(
    query_proj, key_proj, value_proj, grad_out, out_proj, filters, skip_gain, doc_lengths, group_of
):
    tokens, channels = query_proj.shape
    groups = filters.shape[0]
    per_group = channels // groups
    spans = lax.axis_size("ctx")
    heads = lax.axis_size("head")
    position = lax.axis_index("ctx")
    head = lax.axis_index("head")
    sub = channels // spans
    sub_groups = sub // per_group
    lags = (spans // 2 + 1) * tokens
    feats = grad_out.shape[1]
    dma = pltpu.SemaphoreType.DMA
    wide = pltpu.VMEM((tokens, channels), BF16)
    column = pltpu.VMEM((channels, LANES), I32)

    arrived = [lax.ppermute(grad_out, "head", [(i, (i + r) % heads) for i in range(heads)]) for r in range(1, heads)]

    gate_sorted, rank = call(
        functools.partial(gate_kernel, groups=groups, per_group=per_group),
        (pltpu.VMEM((spans, sub, tokens), BF16), pltpu.VMEM((1, channels), I32)),
        [SMEM, VMEM, ANY, ANY],
        [wide, wide, column, dma((2,))],
    )(head.reshape(1), group_of.reshape(1, channels), query_proj, key_proj)
    gate_moved = lax.all_to_all(gate_sorted, "ctx", 0, 0)

    parts = min(8, feats // LANES)
    acc = None
    for r, grad in enumerate([grad_out] + arrived):
        source = ((head + heads - r) % heads).reshape(1)
        if r < heads - 1:
            acc = call(
                partial_kernel,
                pltpu.VMEM((tokens, channels), F32),
                [SMEM, ANY, ANY] + ([] if acc is None else [VMEM]),
                [
                    pltpu.VMEM((tokens, feats), BF16),
                    pltpu.VMEM((channels, feats), BF16),
                    dma((parts,)),
                    dma,
                ],
            )(source, grad, out_proj, *([] if acc is None else [acc]))
            acc = on_chip(acc)
        else:
            conv_sorted, conv_grad = call(
                last_kernel,
                (pltpu.VMEM((spans, sub, tokens), BF16), pltpu.VMEM((tokens, channels), BF16)),
                [SMEM, VMEM, VMEM, VMEM, ANY, ANY],
                [
                    pltpu.VMEM((tokens, channels), F32),
                    pltpu.VMEM((channels, feats), BF16),
                    wide,
                    column,
                    dma((parts,)),
                    dma,
                ],
            )(source, on_chip(rank), on_chip(grad), acc, out_proj, value_proj)
    conv_moved = lax.all_to_all(on_chip(conv_sorted), "ctx", 0, 0)

    filt_sub = lax.dynamic_slice(filters, (position * sub_groups, 0), (sub_groups, lags)).astype(F32)
    gate_t, rows, doc, skip = call(
        functools.partial(prepare_kernel, per_group=per_group),
        (
            pltpu.VMEM((sub_groups, tokens, spans * per_group), BF16),
            pltpu.VMEM((sub_groups, lags + tokens), F32),
            pltpu.VMEM((spans * per_group, tokens), F32),
            pltpu.VMEM((1, channels), F32),
        ),
        [SMEM, VMEM, VMEM, VMEM],
    )(doc_lengths, filt_sub, on_chip(gate_moved), skip_gain.reshape(1, channels))

    back = call(
        functools.partial(conv_kernel, per_group=per_group),
        pltpu.VMEM((spans, sub + EXTRA, tokens), BF16),
        [VMEM] * 4,
        [
            pltpu.VMEM((sub_groups, spans * per_group, lags), BF16),
            pltpu.VMEM((EXTRA // 2, lags), F32),
        ],
    )(on_chip(conv_moved), on_chip(gate_t), on_chip(rows), on_chip(doc))
    back_moved = lax.all_to_all(on_chip(back), "ctx", 0, 0)

    return call(
        functools.partial(gates_kernel, sub_groups=sub_groups),
        (
            jax.ShapeDtypeStruct((tokens, channels), BF16),
            jax.ShapeDtypeStruct((tokens, channels), BF16),
            jax.ShapeDtypeStruct((groups, tokens), F32),
        ),
        [VMEM, VMEM, VMEM, VMEM, ANY, ANY],
        [wide, wide, wide, wide, pltpu.VMEM((groups, tokens), F32), wide, dma((2,)), dma((2, 8)), dma],
        (ANY, ANY, ANY),
    )(on_chip(back_moved), on_chip(rank), on_chip(conv_grad), on_chip(skip), query_proj, key_proj)


def solution(mesh):
    in_specs = (
        P("ctx", "head"),
        P("ctx", "head"),
        P("ctx", "head"),
        P("ctx", "head"),
        P("head", None),
        P("head", None),
        P("head"),
        P(),
        P("head"),
    )
    out_specs = (P("ctx", "head"), P("ctx", "head"), P("head", "ctx"))

    def body(*args):
        return tuple(per_device(*args))

    return jax.shard_map(body, mesh=mesh, in_specs=in_specs, out_specs=out_specs, check_vma=False)
```

```python
import functools

import jax
import jax.numpy as jnp
from jax import lax
from jax.experimental import pallas as pl
from jax.experimental.pallas import tpu as pltpu
from jax.sharding import PartitionSpec as P

F32 = jnp.float32
BF16 = jnp.bfloat16
I32 = jnp.int32
NT = (((1,), (1,)), ((), ()))
NN = (((1,), (0,)), ((), ()))
LANES = 128
CHUNKS = 2
EXTRA = 16
VMEM = pl.BlockSpec(memory_space=pltpu.VMEM)
SMEM = pl.BlockSpec(memory_space=pltpu.SMEM)
ANY = pl.BlockSpec(memory_space=pl.ANY)


def dot(a, b, dims):
    return lax.dot_general(a, b, dims, preferred_element_type=F32)


def on_chip(x):
    return pltpu.with_memory_space_constraint(x, pltpu.VMEM)


def call(kernel, out_shape, in_specs, scratch=(), out_specs=None):
    return pl.pallas_call(
        kernel,
        out_shape=out_shape,
        in_specs=in_specs,
        out_specs=jax.tree.map(lambda _: VMEM, out_shape) if out_specs is None else out_specs,
        scratch_shapes=scratch,
        compiler_params=pltpu.CompilerParams(vmem_limit_bytes=56 * 1024 * 1024),
    )


def rank_column(rank_row, column_ref):
    wide = jnp.broadcast_to(rank_row.astype(F32), (LANES, rank_row.shape[1]))
    column_ref[...] = wide.T.astype(I32)


def permute(by_token, column_ref, first, count, store):
    channels = column_ref.shape[0]
    width = min(2 * LANES, count)
    lane = lax.broadcasted_iota(I32, (channels, LANES), 1)
    for p in range(first, first + count, width):
        picks = [
            jnp.where(column_ref[...] == lane + (p + q), 1.0, 0.0).astype(BF16)
            for q in range(0, width, LANES)
        ]
        store(p, dot(by_token, jnp.concatenate(picks, axis=1), NN).T.astype(BF16))


def store_chunk(out_ref, start):
    rows = out_ref.shape[1]

    def store(p, block):
        blocks = block.shape[0] // rows
        at = (p - start) // rows
        out_ref[at : at + blocks] = block.reshape(blocks, rows, -1)

    return store


def gate_kernel(
    group_hbm, query_hbm, key_hbm, out_ref, rank_ref, group_ref, query_ref, key_ref, column_ref, sem, *, groups, per_group
):
    loads = [
        pltpu.make_async_copy(group_hbm, group_ref, sem.at[0]),
        pltpu.make_async_copy(query_hbm, query_ref, sem.at[1]),
        pltpu.make_async_copy(key_hbm, key_ref, sem.at[2]),
    ]
    for load in loads:
        load.start()
    channels = group_ref.shape[1]
    spans, sub, tokens = out_ref.shape
    near = (sub // per_group // CHUNKS).bit_length() - 1
    parts = CHUNKS.bit_length() - 1
    upper = lax.broadcasted_iota(I32, (LANES, LANES), 0) < lax.broadcasted_iota(I32, (LANES, LANES), 1)
    upper = jnp.where(upper, 1.0, 0.0).astype(BF16)
    base = jnp.zeros((groups, 1), F32)
    loads[0].wait()
    local = group_ref[...] & (groups - 1)
    order = (local & ((1 << near) - 1)) | ((local >> (near + parts)) << near)
    order = order | (((local >> near) & (CHUNKS - 1)) << (groups.bit_length() - 1 - parts))
    for b in range(channels // LANES):
        cols = slice(b * LANES, (b + 1) * LANES)
        member = jnp.where(lax.broadcasted_iota(I32, (groups, LANES), 0) == order[:, cols], 1.0, 0.0)
        before = dot(member.astype(BF16), upper, NN) + base
        place = jnp.sum(member * before, axis=0, keepdims=True)
        rank_ref[:, cols] = order[:, cols] * per_group + place.astype(I32)
        base = base + jnp.sum(member, axis=1, keepdims=True)
    rank_column(rank_ref[...], column_ref)
    for load in loads[1:]:
        load.wait()
    gated = (query_ref[...].astype(F32) * key_ref[...].astype(F32)).astype(BF16)
    part = sub // CHUNKS

    def store(p, block):
        blocks = block.shape[0] // part
        chunk, at = divmod(p // part, spans)
        out_ref[at : at + blocks, chunk * part : (chunk + 1) * part, :] = block.reshape(blocks, part, tokens)

    permute(gated, column_ref, 0, channels, store)


def stream_weights(half, weight_hbm, weight_ref, sem):
    _, feats = weight_ref.shape
    count = sem.shape[0]
    width = feats // count
    copies = [
        pltpu.make_async_copy(
            weight_hbm.at[:, pl.ds(pl.multiple_of(half * feats + j * width, width), width)],
            weight_ref.at[:, pl.ds(j * width, width)],
            sem.at[j],
        )
        for j in range(count)
    ]
    for copy in copies:
        copy.start()
    return copies, width


def product(copies, width, grad_ref, weight_ref, out_ref, fresh):
    for j, copy in enumerate(copies):
        copy.wait()
        cols = slice(j * width, (j + 1) * width)
        part = dot(grad_ref[:, cols], weight_ref[:, cols], NT)
        out_ref[...] = part if fresh and j == 0 else out_ref[...] + part


def partial_kernel(half_ref, grad_ref, weight_hbm, *refs):
    *acc, out_ref, weight_ref, sem = refs
    copies, width = stream_weights(half_ref[0], weight_hbm, weight_ref, sem)
    if acc:
        out_ref[...] = acc[0][...]
    product(copies, width, grad_ref, weight_ref, out_ref, not acc)


def last_kernel(
    half_ref, rank_ref, grad_ref, acc_ref, weight_hbm, value_hbm, out_ref, conv_ref, total_ref, weight_ref, value_ref, column_ref, sem, value_sem
):
    load = pltpu.make_async_copy(value_hbm, value_ref, value_sem)
    copies, width = stream_weights(half_ref[0], weight_hbm, weight_ref, sem)
    load.start()
    rank_column(rank_ref[...], column_ref)
    total_ref[...] = acc_ref[...]
    product(copies, width, grad_ref, weight_ref, total_ref, False)
    load.wait()
    conv_ref[...] = (total_ref[...] * value_ref[...].astype(F32)).astype(BF16)
    permute(conv_ref[...], column_ref, 0, out_ref.shape[0] * out_ref.shape[1], store_chunk(out_ref, 0))


def more_kernel(rank_ref, conv_ref, out_ref, column_ref, *, chunk):
    rank_column(rank_ref[...], column_ref)
    count = out_ref.shape[0] * out_ref.shape[1]
    permute(conv_ref[...], column_ref, chunk * count, count, store_chunk(out_ref, chunk * count))


def prepare_kernel(docs_ref, filt_ref, gate_ref, skip_ref, gate_t_ref, rows_ref, doc_ref, skip_out_ref, *, per_group):
    spans, _, tokens = gate_ref.shape
    groups, lags = filt_ref.shape
    flip = lax.broadcasted_iota(I32, (tokens, tokens), 0) + lax.broadcasted_iota(I32, (tokens, tokens), 1)
    flip = jnp.where(flip == tokens - 1, 1.0, 0.0).astype(BF16)
    for g in range(groups):
        gate = gate_ref[:, g * per_group : (g + 1) * per_group, :].reshape(spans * per_group, tokens)
        gate_t_ref[g] = dot(flip, gate, NT).astype(BF16)
    rows_ref[:, :lags] = filt_ref[...]
    rows_ref[:, lags:] = jnp.zeros((groups, tokens), F32)
    index = lax.broadcasted_iota(I32, doc_ref.shape, 0) // per_group
    bound = 0
    doc = jnp.zeros(doc_ref.shape, F32)
    for d in range(docs_ref.shape[0]):
        bound = bound + docs_ref[d]
        doc = doc + jnp.where(index >= bound, 1.0, 0.0)
    doc_ref[...] = doc
    skip_out_ref[...] = skip_ref[...]


def conv_kernel(grad_ref, gate_t_ref, rows_ref, doc_ref, *refs, per_group, chunk):
    *earlier, out_ref, sums_ref, moved_ref = refs
    spans, sub, tokens = grad_ref.shape
    groups = sub // per_group
    first = chunk * groups
    padded = rows_ref.shape[1]
    lags = padded - tokens
    reach = lags // tokens
    for k in range(reach):
        cut = k * per_group
        keep = (spans - k) * per_group
        same = jnp.where(doc_ref[cut:, :] == doc_ref[:keep, :], 1.0, 0.0).astype(BF16)
        cols = slice(k * tokens, (k + 1) * tokens)
        for g in range(groups):
            grad = grad_ref[k:, g * per_group : (g + 1) * per_group, :].reshape(keep, tokens)
            moved_ref[g, :keep, cols] = grad * same
            if k:
                moved_ref[g, keep:, cols] = jnp.zeros((cut, tokens), BF16)
    sums_ref[...] = earlier[0][...] if earlier else jnp.zeros(sums_ref.shape, F32)
    for g in range(groups):
        moved = moved_ref[g]
        wide = jnp.broadcast_to(rows_ref[first + g : first + g + 1, :], (tokens, padded))
        toeplitz = pltpu.roll(wide, 0, 1, stride=1, stride_axis=0)[:, :lags].astype(BF16)
        back = dot(moved, toeplitz, NT)
        out_ref[:, g * per_group : (g + 1) * per_group, :] = back.astype(BF16).reshape(spans, per_group, tokens)
        corr = dot(gate_t_ref[first + g], moved, NN)
        wide = jnp.concatenate([corr, jnp.zeros((tokens, tokens), F32)], axis=1)
        skewed = pltpu.roll(wide, lags + 1, 1, stride=1, stride_axis=0)
        sums_ref[first + g : first + g + 1, :] = jnp.sum(skewed[:, :lags], axis=0, keepdims=True)
    if out_ref.shape[1] == sub:
        return
    for k in range(spans):
        if k < reach:
            exact = sums_ref[:, k * tokens : (k + 1) * tokens]
            high = exact.astype(BF16).astype(F32)
            both = jnp.concatenate([high, exact - high], axis=0).astype(BF16)
        else:
            both = jnp.zeros((EXTRA, tokens), BF16)
        out_ref[k, sub:, :] = both


def restore_kernel(back_ref, rank_ref, conv_ref, skip_ref, *refs, chunk):
    *acc, out_ref, sorted_ref = refs
    spans, rows, tokens = back_ref.shape
    count = spans * rows
    sorted_ref[...] = back_ref[...].reshape(count, tokens).T
    channels = rank_ref.shape[1]
    width = min(2 * LANES, channels)
    for j in range(0, channels, width):
        cols = slice(j, j + width)
        picks = lax.broadcasted_iota(I32, (count, width), 0) == rank_ref[:, cols] - chunk * count
        more = dot(sorted_ref[...], jnp.where(picks, 1.0, 0.0).astype(BF16), NN)
        out_ref[:, cols] = more + (acc[0][:, cols] if acc else conv_ref[:, cols].astype(F32) * skip_ref[:, cols])


def gates_kernel(
    back_ref, rank_ref, acc_ref, query_hbm, key_hbm, grad_query_hbm, grad_key_hbm, filt_hbm,
    query_ref, key_ref, grad_query_ref, grad_key_ref, filt_ref, sorted_ref, load_sem, store_sem, filt_sem, *, sub_groups
):
    spans, rows, tokens = back_ref.shape
    sub = rows - EXTRA
    count = spans * sub
    channels = rank_ref.shape[1]
    loads = [
        pltpu.make_async_copy(query_hbm, query_ref, load_sem.at[0]),
        pltpu.make_async_copy(key_hbm, key_ref, load_sem.at[1]),
    ]
    for load in loads:
        load.start()
    sorted_ref[...] = back_ref[:, :sub, :].reshape(count, tokens).T
    for d in range(spans):
        tail = back_ref[d, sub:, :].astype(F32)
        both = tail[: EXTRA // 2] + tail[EXTRA // 2 :]
        filt_ref[d * sub_groups : (d + 1) * sub_groups, :] = both[:sub_groups]
    stores = [pltpu.make_async_copy(filt_ref, filt_hbm, filt_sem)]
    stores[0].start()
    for load in loads:
        load.wait()
    width = channels // store_sem.shape[1]
    for j in range(store_sem.shape[1]):
        cols = slice(j * width, (j + 1) * width)
        picks = lax.broadcasted_iota(I32, (count, width), 0) == rank_ref[:, cols] - (CHUNKS - 1) * count
        gated_grad = acc_ref[:, cols] + dot(sorted_ref[...], jnp.where(picks, 1.0, 0.0).astype(BF16), NN)
        grad_query_ref[:, cols] = (gated_grad * key_ref[:, cols].astype(F32)).astype(BF16)
        grad_key_ref[:, cols] = (gated_grad * query_ref[:, cols].astype(F32)).astype(BF16)
        for which, (source, target) in enumerate(((grad_query_ref, grad_query_hbm), (grad_key_ref, grad_key_hbm))):
            part = pl.ds(j * width, width)
            stores.append(pltpu.make_async_copy(source.at[:, part], target.at[:, part], store_sem.at[which, j]))
            stores[-1].start()
    for store in stores:
        store.wait()


def per_device(
    query_proj, key_proj, value_proj, grad_out, out_proj, filters, skip_gain, doc_lengths, group_of
):
    tokens, channels = query_proj.shape
    groups = filters.shape[0]
    per_group = channels // groups
    spans = lax.axis_size("ctx")
    heads = lax.axis_size("head")
    position = lax.axis_index("ctx")
    head = lax.axis_index("head")
    sub = channels // spans
    sub_groups = sub // per_group
    part = sub // CHUNKS
    lags = (spans // 2 + 1) * tokens
    feats = grad_out.shape[1]
    dma = pltpu.SemaphoreType.DMA
    wide = pltpu.VMEM((tokens, channels), BF16)
    column = pltpu.VMEM((channels, LANES), I32)

    arrived = [lax.ppermute(grad_out, "head", [(i, (i + r) % heads) for i in range(heads)]) for r in range(1, heads)]

    gate_sorted, rank = call(
        functools.partial(gate_kernel, groups=groups, per_group=per_group),
        (pltpu.VMEM((spans, sub, tokens), BF16), pltpu.VMEM((1, channels), I32)),
        [ANY, ANY, ANY],
        [pltpu.VMEM((1, channels), I32), wide, wide, column, dma((3,))],
    )(group_of.reshape(1, channels), query_proj, key_proj)
    rank = on_chip(rank)
    gate_moved = lax.all_to_all(on_chip(gate_sorted), "ctx", 0, 0)

    parts = min(8, feats // LANES)
    streams = [pltpu.VMEM((channels, feats), BF16)]
    acc = None
    for r, grad in enumerate([grad_out] + arrived):
        source = ((head + heads - r) % heads).reshape(1)
        if r < heads - 1:
            acc = call(
                partial_kernel,
                pltpu.VMEM((tokens, channels), F32),
                [SMEM, VMEM, ANY] + ([] if acc is None else [VMEM]),
                streams + [dma((parts,))],
            )(source, on_chip(grad), out_proj, *([] if acc is None else [acc]))
            acc = on_chip(acc)
        else:
            conv_sorted, conv_grad = call(
                last_kernel,
                (pltpu.VMEM((spans, part, tokens), BF16), pltpu.VMEM((tokens, channels), BF16)),
                [SMEM, VMEM, VMEM, VMEM, ANY, ANY],
                [pltpu.VMEM((tokens, channels), F32)] + streams + [wide, column, dma((parts,)), dma],
            )(source, rank, on_chip(grad), acc, out_proj, value_proj)
            conv_grad = on_chip(conv_grad)

    conv_moved = []
    for q in range(CHUNKS):
        if q:
            conv_sorted = call(
                functools.partial(more_kernel, chunk=q), pltpu.VMEM((spans, part, tokens), BF16), [VMEM, VMEM], [column]
            )(rank, conv_grad)
        conv_moved.append(lax.all_to_all(on_chip(conv_sorted), "ctx", 0, 0))

    filt_sub = lax.dynamic_slice(filters, (position * sub_groups, 0), (sub_groups, lags)).astype(F32)
    gate_t, rows, doc, skip = call(
        functools.partial(prepare_kernel, per_group=per_group),
        (
            pltpu.VMEM((sub_groups, tokens, spans * per_group), BF16),
            pltpu.VMEM((sub_groups, lags + tokens), F32),
            pltpu.VMEM((spans * per_group, tokens), F32),
            pltpu.VMEM((1, channels), F32),
        ),
        [SMEM, VMEM, VMEM, VMEM],
    )(doc_lengths, filt_sub, on_chip(gate_moved), skip_gain.reshape(1, channels))
    gate_t, rows, doc, skip = on_chip(gate_t), on_chip(rows), on_chip(doc), on_chip(skip)

    back_moved = []
    sums = []
    for q in range(CHUNKS):
        final = q == CHUNKS - 1
        back, total = call(
            functools.partial(conv_kernel, per_group=per_group, chunk=q),
            (pltpu.VMEM((spans, part + (EXTRA if final else 0), tokens), BF16), pltpu.VMEM((EXTRA // 2, lags), F32)),
            [VMEM] * (4 + len(sums)),
            [pltpu.VMEM((part // per_group, spans * per_group, lags), BF16)],
        )(on_chip(conv_moved[q]), gate_t, rows, doc, *sums)
        sums = [on_chip(total)]
        back_moved.append(lax.all_to_all(on_chip(back), "ctx", 0, 0))

    restored = []
    for q in range(CHUNKS - 1):
        restored = [
            on_chip(
                call(
                    functools.partial(restore_kernel, chunk=q),
                    pltpu.VMEM((tokens, channels), F32),
                    [VMEM] * (4 + len(restored)),
                    [pltpu.VMEM((tokens, spans * part), BF16)],
                )(on_chip(back_moved[q]), rank, conv_grad, skip, *restored)
            )
        ]
    return call(
        functools.partial(gates_kernel, sub_groups=sub_groups),
        (
            jax.ShapeDtypeStruct((tokens, channels), BF16),
            jax.ShapeDtypeStruct((tokens, channels), BF16),
            jax.ShapeDtypeStruct((groups, tokens), F32),
        ),
        [VMEM, VMEM, VMEM, ANY, ANY],
        [wide, wide, wide, wide, pltpu.VMEM((groups, tokens), F32)]
        + [pltpu.VMEM((tokens, spans * part), BF16), dma((2,)), dma((2, min(8, channels // LANES))), dma],
        (ANY, ANY, ANY),
    )(on_chip(back_moved[-1]), rank, *restored, query_proj, key_proj)


def solution(mesh):
    in_specs = (
        P("ctx", "head"),
        P("ctx", "head"),
        P("ctx", "head"),
        P("ctx", "head"),
        P("head", None),
        P("head", None),
        P("head"),
        P(),
        P("head"),
    )
    out_specs = (P("ctx", "head"), P("ctx", "head"), P("head", "ctx"))

    def body(*args):
        return tuple(per_device(*args))

    return jax.shard_map(body, mesh=mesh, in_specs=in_specs, out_specs=out_specs, check_vma=False)
```

```python
import functools

import jax
import jax.numpy as jnp
from jax import lax
from jax.experimental import pallas as pl
from jax.experimental.pallas import tpu as pltpu
from jax.sharding import PartitionSpec as P

F32 = jnp.float32
BF16 = jnp.bfloat16
I32 = jnp.int32
NT = (((1,), (1,)), ((), ()))
NN = (((1,), (0,)), ((), ()))
LANES = 128
EXTRA = 8
VMEM = pl.BlockSpec(memory_space=pltpu.VMEM)
SMEM = pl.BlockSpec(memory_space=pltpu.SMEM)
ANY = pl.BlockSpec(memory_space=pl.ANY)


def dot(a, b, dims):
    return lax.dot_general(a, b, dims, preferred_element_type=F32)


def on_chip(x):
    return pltpu.with_memory_space_constraint(x, pltpu.VMEM)


def call(kernel, out_shape, in_specs, scratch=(), out_specs=None):
    return pl.pallas_call(
        kernel,
        out_shape=out_shape,
        in_specs=in_specs,
        out_specs=jax.tree.map(lambda _: VMEM, out_shape) if out_specs is None else out_specs,
        scratch_shapes=scratch,
        compiler_params=pltpu.CompilerParams(vmem_limit_bytes=56 * 1024 * 1024),
    )


def rank_column(rank_row, column_ref):
    wide = jnp.broadcast_to(rank_row.astype(F32), (LANES, rank_row.shape[1]))
    column_ref[...] = wide.T.astype(I32)


def permute(by_token, column_ref, out_ref):
    channels = column_ref.shape[0]
    rows = out_ref.shape[1]
    width = min(2 * LANES, channels)
    lane = lax.broadcasted_iota(I32, (channels, LANES), 1)
    for p in range(0, channels, width):
        picks = [
            jnp.where(column_ref[...] == lane + (p + q), 1.0, 0.0).astype(BF16)
            for q in range(0, width, LANES)
        ]
        moved = dot(by_token, jnp.concatenate(picks, axis=1), NN).T.astype(BF16)
        out_ref[p // rows : (p + width) // rows] = moved.reshape(width // rows, rows, -1)


def gate_kernel(
    group_hbm, query_hbm, key_hbm, grad_hbm, out_ref, rank_ref, grad_ref, group_ref, query_ref, key_ref, column_ref, sem, *, groups, per_group
):
    loads = [
        pltpu.make_async_copy(group_hbm, group_ref, sem.at[0]),
        pltpu.make_async_copy(query_hbm, query_ref, sem.at[1]),
        pltpu.make_async_copy(key_hbm, key_ref, sem.at[2]),
        pltpu.make_async_copy(grad_hbm, grad_ref, sem.at[3]),
    ]
    for load in loads:
        load.start()
    channels = group_ref.shape[1]
    upper = lax.broadcasted_iota(I32, (LANES, LANES), 0) < lax.broadcasted_iota(I32, (LANES, LANES), 1)
    upper = jnp.where(upper, 1.0, 0.0).astype(BF16)
    base = jnp.zeros((groups, 1), F32)
    loads[0].wait()
    local = group_ref[...] & (groups - 1)
    for b in range(channels // LANES):
        here = local[:, b * LANES : (b + 1) * LANES]
        member = jnp.where(lax.broadcasted_iota(I32, (groups, LANES), 0) == here, 1.0, 0.0)
        before = dot(member.astype(BF16), upper, NN) + base
        place = jnp.sum(member * before, axis=0, keepdims=True)
        rank_ref[:, b * LANES : (b + 1) * LANES] = here * per_group + place.astype(I32)
        base = base + jnp.sum(member, axis=1, keepdims=True)
    rank_column(rank_ref[...], column_ref)
    for load in loads[1:3]:
        load.wait()
    gated = (query_ref[...].astype(F32) * key_ref[...].astype(F32)).astype(BF16)
    permute(gated, column_ref, out_ref)
    loads[3].wait()


def stream_weights(half, weight_hbm, weight_ref, sem):
    _, feats = weight_ref.shape
    count = sem.shape[0]
    width = feats // count
    copies = [
        pltpu.make_async_copy(
            weight_hbm.at[:, pl.ds(pl.multiple_of(half * feats + j * width, width), width)],
            weight_ref.at[:, pl.ds(j * width, width)],
            sem.at[j],
        )
        for j in range(count)
    ]
    for copy in copies:
        copy.start()
    return copies, width


def product(copies, width, grad_ref, weight_ref, out_ref, fresh):
    for j, copy in enumerate(copies):
        copy.wait()
        cols = slice(j * width, (j + 1) * width)
        part = dot(grad_ref[:, cols], weight_ref[:, cols], NT)
        out_ref[...] = part if fresh and j == 0 else out_ref[...] + part


def partial_kernel(half_ref, grad_ref, weight_hbm, *refs):
    *acc, out_ref, weight_ref, sem = refs
    copies, width = stream_weights(half_ref[0], weight_hbm, weight_ref, sem)
    if acc:
        out_ref[...] = acc[0][...]
    product(copies, width, grad_ref, weight_ref, out_ref, not acc)


def last_kernel(
    half_ref, rank_ref, grad_ref, acc_ref, weight_hbm, value_hbm, out_ref, conv_ref, total_ref, weight_ref, value_ref, column_ref, sem, value_sem
):
    load = pltpu.make_async_copy(value_hbm, value_ref, value_sem)
    copies, width = stream_weights(half_ref[0], weight_hbm, weight_ref, sem)
    load.start()
    rank_column(rank_ref[...], column_ref)
    total_ref[...] = acc_ref[...]
    product(copies, width, grad_ref, weight_ref, total_ref, False)
    load.wait()
    conv_ref[...] = (total_ref[...] * value_ref[...].astype(F32)).astype(BF16)
    permute(conv_ref[...], column_ref, out_ref)


def prepare_kernel(docs_ref, filt_ref, gate_ref, skip_ref, gate_t_ref, rows_ref, doc_ref, skip_out_ref, *, per_group):
    spans, _, tokens = gate_ref.shape
    groups, lags = filt_ref.shape
    flip = lax.broadcasted_iota(I32, (tokens, tokens), 0) + lax.broadcasted_iota(I32, (tokens, tokens), 1)
    flip = jnp.where(flip == tokens - 1, 1.0, 0.0).astype(BF16)
    for g in range(groups):
        gate = gate_ref[:, g * per_group : (g + 1) * per_group, :].reshape(spans * per_group, tokens)
        gate_t_ref[g] = dot(flip, gate, NT).astype(BF16)
    rows_ref[:, :lags] = filt_ref[...]
    rows_ref[:, lags:] = jnp.zeros((groups, tokens), F32)
    index = lax.broadcasted_iota(I32, doc_ref.shape, 0) // per_group
    bound = 0
    doc = jnp.zeros(doc_ref.shape, F32)
    for d in range(docs_ref.shape[0]):
        bound = bound + docs_ref[d]
        doc = doc + jnp.where(index >= bound, 1.0, 0.0)
    doc_ref[...] = doc
    skip_out_ref[...] = skip_ref[...]


def conv_kernel(grad_ref, gate_t_ref, rows_ref, doc_ref, out_ref, moved_ref, sums_ref, *, per_group):
    spans, sub, tokens = grad_ref.shape
    groups, padded = rows_ref.shape
    lags = padded - tokens
    reach = lags // tokens
    for k in range(reach):
        cut = k * per_group
        keep = (spans - k) * per_group
        same = jnp.where(doc_ref[cut:, :] == doc_ref[:keep, :], 1.0, 0.0).astype(BF16)
        cols = slice(k * tokens, (k + 1) * tokens)
        for g in range(groups):
            grad = grad_ref[k:, g * per_group : (g + 1) * per_group, :].reshape(keep, tokens)
            moved_ref[g, :keep, cols] = grad * same
            if k:
                moved_ref[g, keep:, cols] = jnp.zeros((cut, tokens), BF16)
    sums_ref[...] = jnp.zeros(sums_ref.shape, F32)
    for g in range(groups):
        moved = moved_ref[g]
        wide = jnp.broadcast_to(rows_ref[g : g + 1, :], (tokens, padded))
        toeplitz = pltpu.roll(wide, 0, 1, stride=1, stride_axis=0)[:, :lags].astype(BF16)
        back = dot(moved, toeplitz, NT)
        out_ref[:, g * per_group : (g + 1) * per_group, :] = back.astype(BF16).reshape(spans, per_group, tokens)
        corr = dot(gate_t_ref[g], moved, NN)
        wide = jnp.concatenate([corr, jnp.zeros((tokens, tokens), F32)], axis=1)
        skewed = pltpu.roll(wide, lags + 1, 1, stride=1, stride_axis=0)
        sums_ref[g : g + 1, :] = jnp.sum(skewed[:, :lags], axis=0, keepdims=True)
    for k in range(spans):
        if k < reach:
            out_ref[k, sub:, :] = sums_ref[:, k * tokens : (k + 1) * tokens].astype(BF16)
        else:
            out_ref[k, sub:, :] = jnp.zeros((EXTRA, tokens), BF16)


def fetch_kernel(query_hbm, key_hbm, query_ref, key_ref, sem):
    loads = [
        pltpu.make_async_copy(query_hbm, query_ref, sem.at[0]),
        pltpu.make_async_copy(key_hbm, key_ref, sem.at[1]),
    ]
    for load in loads:
        load.start()
    for load in loads:
        load.wait()


def gates_kernel(
    back_ref, rank_ref, conv_ref, skip_ref, query_ref, key_ref, grad_query_hbm, grad_key_hbm, filt_hbm,
    grad_query_ref, grad_key_ref, filt_ref, sorted_ref, store_sem, filt_sem, *, sub_groups
):
    spans, rows, tokens = back_ref.shape
    sub = rows - EXTRA
    channels = rank_ref.shape[1]
    sorted_ref[...] = back_ref[:, :sub, :].reshape(spans * sub, tokens).T
    for d in range(spans):
        filt_ref[d * sub_groups : (d + 1) * sub_groups, :] = back_ref[d, sub:, :].astype(F32)[:sub_groups]
    stores = [pltpu.make_async_copy(filt_ref, filt_hbm, filt_sem)]
    stores[0].start()
    width = channels // store_sem.shape[1]
    for j in range(store_sem.shape[1]):
        cols = slice(j * width, (j + 1) * width)
        place = lax.broadcasted_iota(I32, (channels, width), 0)
        picks = jnp.where(place == rank_ref[:, cols], 1.0, 0.0).astype(BF16)
        gated_grad = dot(sorted_ref[...], picks, NN) + conv_ref[:, cols].astype(F32) * skip_ref[:, cols]
        grad_query_ref[:, cols] = (gated_grad * key_ref[:, cols].astype(F32)).astype(BF16)
        grad_key_ref[:, cols] = (gated_grad * query_ref[:, cols].astype(F32)).astype(BF16)
        for which, (source, target) in enumerate(((grad_query_ref, grad_query_hbm), (grad_key_ref, grad_key_hbm))):
            part = pl.ds(j * width, width)
            stores.append(pltpu.make_async_copy(source.at[:, part], target.at[:, part], store_sem.at[which, j]))
            stores[-1].start()
    for store in stores:
        store.wait()


def per_device(
    query_proj, key_proj, value_proj, grad_out, out_proj, filters, skip_gain, doc_lengths, group_of
):
    tokens, channels = query_proj.shape
    groups = filters.shape[0]
    per_group = channels // groups
    spans = lax.axis_size("ctx")
    heads = lax.axis_size("head")
    position = lax.axis_index("ctx")
    head = lax.axis_index("head")
    sub = channels // spans
    sub_groups = sub // per_group
    lags = (spans // 2 + 1) * tokens
    feats = grad_out.shape[1]
    dma = pltpu.SemaphoreType.DMA
    wide = pltpu.VMEM((tokens, channels), BF16)
    column = pltpu.VMEM((channels, LANES), I32)

    arrived = [lax.ppermute(grad_out, "head", [(i, (i + r) % heads) for i in range(heads)]) for r in range(1, heads)]

    gate_sorted, rank, grad_here = call(
        functools.partial(gate_kernel, groups=groups, per_group=per_group),
        (
            pltpu.VMEM((spans, sub, tokens), BF16),
            pltpu.VMEM((1, channels), I32),
            pltpu.VMEM((tokens, feats), BF16),
        ),
        [ANY, ANY, ANY, ANY],
        [pltpu.VMEM((1, channels), I32), wide, wide, column, dma((4,))],
    )(group_of.reshape(1, channels), query_proj, key_proj, grad_out)
    gate_moved = lax.all_to_all(gate_sorted, "ctx", 0, 0)

    parts = min(8, feats // LANES)
    acc = None
    for r, grad in enumerate([grad_here] + arrived):
        source = ((head + heads - r) % heads).reshape(1)
        if r < heads - 1:
            acc = call(
                partial_kernel,
                pltpu.VMEM((tokens, channels), F32),
                [SMEM, VMEM, ANY] + ([] if acc is None else [VMEM]),
                [pltpu.VMEM((channels, feats), BF16), dma((parts,))],
            )(source, on_chip(grad), out_proj, *([] if acc is None else [acc]))
            acc = on_chip(acc)
        else:
            conv_sorted, conv_grad = call(
                last_kernel,
                (pltpu.VMEM((spans, sub, tokens), BF16), pltpu.VMEM((tokens, channels), BF16)),
                [SMEM, VMEM, VMEM, VMEM, ANY, ANY],
                [
                    pltpu.VMEM((tokens, channels), F32),
                    pltpu.VMEM((channels, feats), BF16),
                    wide,
                    column,
                    dma((parts,)),
                    dma,
                ],
            )(source, on_chip(rank), on_chip(grad), acc, out_proj, value_proj)
    conv_moved = lax.all_to_all(on_chip(conv_sorted), "ctx", 0, 0)

    filt_sub = lax.dynamic_slice(filters, (position * sub_groups, 0), (sub_groups, lags)).astype(F32)
    gate_t, rows, doc, skip = call(
        functools.partial(prepare_kernel, per_group=per_group),
        (
            pltpu.VMEM((sub_groups, tokens, spans * per_group), BF16),
            pltpu.VMEM((sub_groups, lags + tokens), F32),
            pltpu.VMEM((spans * per_group, tokens), F32),
            pltpu.VMEM((1, channels), F32),
        ),
        [SMEM, VMEM, VMEM, VMEM],
    )(doc_lengths, filt_sub, on_chip(gate_moved), skip_gain.reshape(1, channels))

    back = call(
        functools.partial(conv_kernel, per_group=per_group),
        pltpu.VMEM((spans, sub + EXTRA, tokens), BF16),
        [VMEM] * 4,
        [
            pltpu.VMEM((sub_groups, spans * per_group, lags), BF16),
            pltpu.VMEM((EXTRA, lags), F32),
        ],
    )(on_chip(conv_moved), on_chip(gate_t), on_chip(rows), on_chip(doc))
    query_here, key_here = call(fetch_kernel, (wide, wide), [ANY, ANY], [dma((2,))])(query_proj, key_proj)
    back_moved = lax.all_to_all(on_chip(back), "ctx", 0, 0)

    return call(
        functools.partial(gates_kernel, sub_groups=sub_groups),
        (
            jax.ShapeDtypeStruct((tokens, channels), BF16),
            jax.ShapeDtypeStruct((tokens, channels), BF16),
            jax.ShapeDtypeStruct((groups, tokens), F32),
        ),
        [VMEM] * 6,
        [wide, wide, pltpu.VMEM((groups, tokens), F32), wide, dma((2, min(8, channels // LANES))), dma],
        (ANY, ANY, ANY),
    )(
        on_chip(back_moved),
        on_chip(rank),
        on_chip(conv_grad),
        on_chip(skip),
        on_chip(query_here),
        on_chip(key_here),
    )


def solution(mesh):
    in_specs = (
        P("ctx", "head"),
        P("ctx", "head"),
        P("ctx", "head"),
        P("ctx", "head"),
        P("head", None),
        P("head", None),
        P("head"),
        P(),
        P("head"),
    )
    out_specs = (P("ctx", "head"), P("ctx", "head"), P("head", "ctx"))

    def body(*args):
        return tuple(per_device(*args))

    return jax.shard_map(body, mesh=mesh, in_specs=in_specs, out_specs=out_specs, check_vma=False)
```

```python
import functools

import jax
import jax.numpy as jnp
from jax import lax
from jax.experimental import pallas as pl
from jax.experimental.pallas import tpu as pltpu
from jax.sharding import PartitionSpec as P

F32 = jnp.float32
BF16 = jnp.bfloat16
I32 = jnp.int32
NT = (((1,), (1,)), ((), ()))
NN = (((1,), (0,)), ((), ()))
LANES = 128
EXTRA = 8
VMEM = pl.BlockSpec(memory_space=pltpu.VMEM)
SMEM = pl.BlockSpec(memory_space=pltpu.SMEM)
ANY = pl.BlockSpec(memory_space=pl.ANY)


def dot(a, b, dims):
    return lax.dot_general(a, b, dims, preferred_element_type=F32)


def on_chip(x):
    return pltpu.with_memory_space_constraint(x, pltpu.VMEM)


def call(kernel, out_shape, in_specs, scratch=(), out_specs=None):
    return pl.pallas_call(
        kernel,
        out_shape=out_shape,
        in_specs=in_specs,
        out_specs=jax.tree.map(lambda _: VMEM, out_shape) if out_specs is None else out_specs,
        scratch_shapes=scratch,
        compiler_params=pltpu.CompilerParams(vmem_limit_bytes=56 * 1024 * 1024),
    )


def rank_column(rank_row, column_ref):
    wide = jnp.broadcast_to(rank_row.astype(F32), (LANES, rank_row.shape[1]))
    column_ref[...] = wide.T.astype(I32)


def permute(by_token, column_ref, starts, width, store):
    channels = column_ref.shape[0]
    lane = lax.broadcasted_iota(I32, (channels, LANES), 1)
    unit = min(width, LANES)
    per_dot = max(1, 2 * LANES // width)
    for i in range(0, len(starts), per_dot):
        picks = []
        for start in starts[i : i + per_dot]:
            for q in range(0, width, unit):
                picks.append((start + q, unit))
        mats = []
        per_tile = LANES // unit
        for j in range(0, len(picks), per_tile):
            want = lane + picks[j][0]
            for t in range(1, per_tile):
                want = jnp.where(lane >= t * unit, lane + (picks[j + t][0] - t * unit), want)
            mats.append(jnp.where(column_ref[...] == want, 1.0, 0.0).astype(BF16))
        moved = dot(by_token, jnp.concatenate(mats, axis=1), NN).T.astype(BF16)
        for j in range(min(per_dot, len(starts) - i)):
            store(i + j, moved[j * width : (j + 1) * width])


def split_pair(ctx, full_ref, mine_ref, other_ref):
    place = ctx & 1
    pair = ctx >> 1
    for p in range(mine_ref.shape[0]):
        mine_ref[pair ^ p] = full_ref[2 * p + place]
        other_ref[pair ^ p] = full_ref[2 * p + 1 - place]


def distances(count):
    ring = count // 4

    def hops(e):
        return (e & 1) + min(e >> 1, ring - (e >> 1))

    return [0] + sorted(range(1, count // 2), key=lambda e: (-hops(e), -(e == 4), e))


def join_pair(ctx, packs, full_ref):
    for e, pack in zip(distances(2 * len(packs)), packs):
        full_ref[ctx ^ (2 * e)] = pack[0]
        full_ref[ctx ^ (2 * e + 1)] = pack[1]


def pack_kernel(mine_ref, got_ref, *packs):
    for e, pack in zip(distances(2 * len(packs)), packs):
        pack[0] = mine_ref[e]
        pack[1] = got_ref[e]


def exchange(mine, swap_other, count):
    got = lax.ppermute(on_chip(swap_other), "ctx", [(i, i ^ 1) for i in range(count)])
    mine = mine()
    shape = pltpu.VMEM((2,) + mine.shape[1:], BF16)
    packs = call(pack_kernel, (shape,) * (count // 2), [VMEM, VMEM])(
        on_chip(mine), on_chip(got)
    )
    out = []
    for e, pack in zip(distances(count), packs):
        moved = lax.ppermute(on_chip(pack), "ctx", [(i, i ^ (2 * e)) for i in range(count)]) if e else pack
        out.append(on_chip(moved))
    return out


def gate_kernel(
    group_hbm, query_hbm, key_hbm, grad_hbm, out_ref, rank_ref, grad_ref, group_ref, query_ref, key_ref, column_ref, sem, *, groups, per_group
):
    loads = [
        pltpu.make_async_copy(group_hbm, group_ref, sem.at[0]),
        pltpu.make_async_copy(query_hbm, query_ref, sem.at[1]),
        pltpu.make_async_copy(key_hbm, key_ref, sem.at[2]),
        pltpu.make_async_copy(grad_hbm, grad_ref, sem.at[3]),
    ]
    for load in loads:
        load.start()
    channels = group_ref.shape[1]
    upper = lax.broadcasted_iota(I32, (LANES, LANES), 0) < lax.broadcasted_iota(I32, (LANES, LANES), 1)
    upper = jnp.where(upper, 1.0, 0.0).astype(BF16)
    base = jnp.zeros((groups, 1), F32)
    loads[0].wait()
    local = group_ref[...] & (groups - 1)
    for b in range(channels // LANES):
        here = local[:, b * LANES : (b + 1) * LANES]
        member = jnp.where(lax.broadcasted_iota(I32, (groups, LANES), 0) == here, 1.0, 0.0)
        before = dot(member.astype(BF16), upper, NN) + base
        place = jnp.sum(member * before, axis=0, keepdims=True)
        rank_ref[:, b * LANES : (b + 1) * LANES] = here * per_group + place.astype(I32)
        base = base + jnp.sum(member, axis=1, keepdims=True)
    rank_column(rank_ref[...], column_ref)
    for load in loads[1:3]:
        load.wait()
    gated = (query_ref[...].astype(F32) * key_ref[...].astype(F32)).astype(BF16)
    rows = out_ref.shape[1]

    def store(i, block):
        out_ref[i] = block

    permute(gated, column_ref, range(0, channels, rows), rows, store)
    loads[3].wait()


def stream_weights(half, weight_hbm, weight_ref, sem):
    _, feats = weight_ref.shape
    count = sem.shape[0]
    width = feats // count
    copies = [
        pltpu.make_async_copy(
            weight_hbm.at[:, pl.ds(pl.multiple_of(half * feats + j * width, width), width)],
            weight_ref.at[:, pl.ds(j * width, width)],
            sem.at[j],
        )
        for j in range(count)
    ]
    for copy in copies:
        copy.start()
    return copies, width


def product(copies, width, grad_ref, weight_ref, out_ref, fresh):
    for j, copy in enumerate(copies):
        copy.wait()
        cols = slice(j * width, (j + 1) * width)
        part = dot(grad_ref[:, cols], weight_ref[:, cols], NT)
        out_ref[...] = part if fresh and j == 0 else out_ref[...] + part


def partial_kernel(half_ref, grad_ref, weight_hbm, *refs):
    *acc, out_ref, weight_ref, sem = refs
    copies, width = stream_weights(half_ref[0], weight_hbm, weight_ref, sem)
    if acc:
        out_ref[...] = acc[0][...]
    product(copies, width, grad_ref, weight_ref, out_ref, not acc)


def pair_blocks(ctx, place, by_token, column_ref, out_ref):
    pairs, rows, _ = out_ref.shape

    def store(p, block):
        out_ref[(ctx >> 1) ^ p] = block

    permute(by_token, column_ref, [(2 * p + place) * rows for p in range(pairs)], rows, store)


def last_kernel(
    half_ref, ctx_ref, rank_ref, grad_ref, acc_ref, weight_hbm, value_hbm, out_ref, conv_ref, total_ref, weight_ref, value_ref, column_ref, sem, value_sem
):
    load = pltpu.make_async_copy(value_hbm, value_ref, value_sem)
    copies, width = stream_weights(half_ref[0], weight_hbm, weight_ref, sem)
    load.start()
    rank_column(rank_ref[...], column_ref)
    total_ref[...] = acc_ref[...]
    product(copies, width, grad_ref, weight_ref, total_ref, False)
    load.wait()
    conv_ref[...] = (total_ref[...] * value_ref[...].astype(F32)).astype(BF16)
    ctx = ctx_ref[0]
    pair_blocks(ctx, 1 - (ctx & 1), conv_ref[...], column_ref, out_ref)


def mine_kernel(ctx_ref, rank_ref, conv_ref, out_ref, column_ref):
    rank_column(rank_ref[...], column_ref)
    ctx = ctx_ref[0]
    pair_blocks(ctx, ctx & 1, conv_ref[...], column_ref, out_ref)


def prepare_kernel(docs_ref, filt_ref, gate_ref, skip_ref, gate_t_ref, rows_ref, doc_ref, skip_out_ref, *, per_group):
    spans, _, tokens = gate_ref.shape
    groups, lags = filt_ref.shape
    flip = lax.broadcasted_iota(I32, (tokens, tokens), 0) + lax.broadcasted_iota(I32, (tokens, tokens), 1)
    flip = jnp.where(flip == tokens - 1, 1.0, 0.0).astype(BF16)
    for g in range(groups):
        gate = gate_ref[:, g * per_group : (g + 1) * per_group, :].reshape(spans * per_group, tokens)
        gate_t_ref[g] = dot(flip, gate, NT).astype(BF16)
    rows_ref[:, :lags] = filt_ref[...]
    rows_ref[:, lags:] = jnp.zeros((groups, tokens), F32)
    index = lax.broadcasted_iota(I32, doc_ref.shape, 0) // per_group
    bound = 0
    doc = jnp.zeros(doc_ref.shape, F32)
    for d in range(docs_ref.shape[0]):
        bound = bound + docs_ref[d]
        doc = doc + jnp.where(index >= bound, 1.0, 0.0)
    doc_ref[...] = doc
    skip_out_ref[...] = skip_ref[...]


def conv_kernel(ctx_ref, gate_t_ref, rows_ref, doc_ref, *refs, per_group):
    *packs, mine_ref, other_ref, grad_ref, out_ref, moved_ref, sums_ref = refs
    join_pair(ctx_ref[0], packs, grad_ref)
    spans, sub, tokens = grad_ref.shape
    groups, padded = rows_ref.shape
    lags = padded - tokens
    reach = lags // tokens
    for k in range(reach):
        cut = k * per_group
        keep = (spans - k) * per_group
        same = jnp.where(doc_ref[cut:, :] == doc_ref[:keep, :], 1.0, 0.0).astype(BF16)
        cols = slice(k * tokens, (k + 1) * tokens)
        for g in range(groups):
            grad = grad_ref[k:, g * per_group : (g + 1) * per_group, :].reshape(keep, tokens)
            moved_ref[g, :keep, cols] = grad * same
            if k:
                moved_ref[g, keep:, cols] = jnp.zeros((cut, tokens), BF16)
    sums_ref[...] = jnp.zeros(sums_ref.shape, F32)
    for g in range(groups):
        moved = moved_ref[g]
        wide = jnp.broadcast_to(rows_ref[g : g + 1, :], (tokens, padded))
        toeplitz = pltpu.roll(wide, 0, 1, stride=1, stride_axis=0)[:, :lags].astype(BF16)
        back = dot(moved, toeplitz, NT)
        out_ref[:, g * per_group : (g + 1) * per_group, :] = back.astype(BF16).reshape(spans, per_group, tokens)
        corr = dot(gate_t_ref[g], moved, NN)
        wide = jnp.concatenate([corr, jnp.zeros((tokens, tokens), F32)], axis=1)
        skewed = pltpu.roll(wide, lags + 1, 1, stride=1, stride_axis=0)
        sums_ref[g : g + 1, :] = jnp.sum(skewed[:, :lags], axis=0, keepdims=True)
    for k in range(spans):
        if k < reach:
            out_ref[k, sub:, :] = sums_ref[:, k * tokens : (k + 1) * tokens].astype(BF16)
        else:
            out_ref[k, sub:, :] = jnp.zeros((EXTRA, tokens), BF16)
    split_pair(ctx_ref[0], out_ref, mine_ref, other_ref)


def fetch_kernel(query_hbm, key_hbm, query_ref, key_ref, sem):
    loads = [
        pltpu.make_async_copy(query_hbm, query_ref, sem.at[0]),
        pltpu.make_async_copy(key_hbm, key_ref, sem.at[1]),
    ]
    for load in loads:
        load.start()
    for load in loads:
        load.wait()


def gates_kernel(
    ctx_ref, rank_ref, conv_ref, skip_ref, query_ref, key_ref, *refs, sub_groups
):
    *packs, grad_query_hbm, grad_key_hbm, filt_hbm = refs[:-7]
    grad_query_ref, grad_key_ref, filt_ref, sorted_ref, back_ref, store_sem, filt_sem = refs[-7:]
    join_pair(ctx_ref[0], packs, back_ref)
    spans, rows, tokens = back_ref.shape
    sub = rows - EXTRA
    channels = rank_ref.shape[1]
    sorted_ref[...] = back_ref[:, :sub, :].reshape(spans * sub, tokens).T
    for d in range(spans):
        filt_ref[d * sub_groups : (d + 1) * sub_groups, :] = back_ref[d, sub:, :].astype(F32)[:sub_groups]
    stores = [pltpu.make_async_copy(filt_ref, filt_hbm, filt_sem)]
    stores[0].start()
    width = channels // store_sem.shape[1]
    for j in range(store_sem.shape[1]):
        cols = slice(j * width, (j + 1) * width)
        place = lax.broadcasted_iota(I32, (channels, width), 0)
        picks = jnp.where(place == rank_ref[:, cols], 1.0, 0.0).astype(BF16)
        gated_grad = dot(sorted_ref[...], picks, NN) + conv_ref[:, cols].astype(F32) * skip_ref[:, cols]
        grad_query_ref[:, cols] = (gated_grad * key_ref[:, cols].astype(F32)).astype(BF16)
        grad_key_ref[:, cols] = (gated_grad * query_ref[:, cols].astype(F32)).astype(BF16)
        for which, (source, target) in enumerate(((grad_query_ref, grad_query_hbm), (grad_key_ref, grad_key_hbm))):
            part = pl.ds(j * width, width)
            stores.append(pltpu.make_async_copy(source.at[:, part], target.at[:, part], store_sem.at[which, j]))
            stores[-1].start()
    for store in stores:
        store.wait()


def per_device(
    query_proj, key_proj, value_proj, grad_out, out_proj, filters, skip_gain, doc_lengths, group_of
):
    tokens, channels = query_proj.shape
    groups = filters.shape[0]
    per_group = channels // groups
    spans = lax.axis_size("ctx")
    heads = lax.axis_size("head")
    position = lax.axis_index("ctx")
    ctx = position.reshape(1)
    head = lax.axis_index("head")
    sub = channels // spans
    sub_groups = sub // per_group
    lags = (spans // 2 + 1) * tokens
    feats = grad_out.shape[1]
    dma = pltpu.SemaphoreType.DMA
    wide = pltpu.VMEM((tokens, channels), BF16)
    column = pltpu.VMEM((channels, LANES), I32)

    arrived = [lax.ppermute(grad_out, "head", [(i, (i + r) % heads) for i in range(heads)]) for r in range(1, heads)]

    gate_sorted, rank, grad_here = call(
        functools.partial(gate_kernel, groups=groups, per_group=per_group),
        (
            pltpu.VMEM((spans, sub, tokens), BF16),
            pltpu.VMEM((1, channels), I32),
            pltpu.VMEM((tokens, feats), BF16),
        ),
        [ANY, ANY, ANY, ANY],
        [pltpu.VMEM((1, channels), I32), wide, wide, column, dma((4,))],
    )(group_of.reshape(1, channels), query_proj, key_proj, grad_out)
    gate_moved = lax.all_to_all(gate_sorted, "ctx", 0, 0)

    parts = min(8, feats // LANES)
    acc = None
    for r, grad in enumerate([grad_here] + arrived):
        source = ((head + heads - r) % heads).reshape(1)
        if r < heads - 1:
            acc = call(
                partial_kernel,
                pltpu.VMEM((tokens, channels), F32),
                [SMEM, VMEM, ANY] + ([] if acc is None else [VMEM]),
                [pltpu.VMEM((channels, feats), BF16), dma((parts,))],
            )(source, on_chip(grad), out_proj, *([] if acc is None else [acc]))
            acc = on_chip(acc)
        else:
            conv_sorted, conv_grad = call(
                last_kernel,
                (pltpu.VMEM((spans // 2, sub, tokens), BF16), pltpu.VMEM((tokens, channels), BF16)),
                [SMEM, SMEM, VMEM, VMEM, VMEM, ANY, ANY],
                [
                    pltpu.VMEM((tokens, channels), F32),
                    pltpu.VMEM((channels, feats), BF16),
                    wide,
                    column,
                    dma((parts,)),
                    dma,
                ],
            )(source, ctx, on_chip(rank), on_chip(grad), acc, out_proj, value_proj)

    def conv_mine():
        return call(
            mine_kernel, pltpu.VMEM((spans // 2, sub, tokens), BF16), [SMEM, VMEM, VMEM], [column]
        )(ctx, on_chip(rank), on_chip(conv_grad))

    conv_moved = exchange(conv_mine, conv_sorted, spans)

    filt_sub = lax.dynamic_slice(filters, (position * sub_groups, 0), (sub_groups, lags)).astype(F32)
    gate_t, rows, doc, skip = call(
        functools.partial(prepare_kernel, per_group=per_group),
        (
            pltpu.VMEM((sub_groups, tokens, spans * per_group), BF16),
            pltpu.VMEM((sub_groups, lags + tokens), F32),
            pltpu.VMEM((spans * per_group, tokens), F32),
            pltpu.VMEM((1, channels), F32),
        ),
        [SMEM, VMEM, VMEM, VMEM],
    )(doc_lengths, filt_sub, on_chip(gate_moved), skip_gain.reshape(1, channels))

    back, back_other = call(
        functools.partial(conv_kernel, per_group=per_group),
        (pltpu.VMEM((spans // 2, sub + EXTRA, tokens), BF16),) * 2,
        [SMEM] + [VMEM] * (3 + spans // 2),
        [
            pltpu.VMEM((spans, sub, tokens), BF16),
            pltpu.VMEM((spans, sub + EXTRA, tokens), BF16),
            pltpu.VMEM((sub_groups, spans * per_group, lags), BF16),
            pltpu.VMEM((EXTRA, lags), F32),
        ],
    )(ctx, on_chip(gate_t), on_chip(rows), on_chip(doc), *conv_moved)
    query_here, key_here = call(fetch_kernel, (wide, wide), [ANY, ANY], [dma((2,))])(query_proj, key_proj)
    back_moved = exchange(lambda: back, back_other, spans)

    return call(
        functools.partial(gates_kernel, sub_groups=sub_groups),
        (
            jax.ShapeDtypeStruct((tokens, channels), BF16),
            jax.ShapeDtypeStruct((tokens, channels), BF16),
            jax.ShapeDtypeStruct((groups, tokens), F32),
        ),
        [SMEM] + [VMEM] * (5 + spans // 2),
        [wide, wide, pltpu.VMEM((groups, tokens), F32), wide]
        + [pltpu.VMEM((spans, sub + EXTRA, tokens), BF16), dma((2, min(8, channels // LANES))), dma],
        (ANY, ANY, ANY),
    )(
        ctx,
        on_chip(rank),
        on_chip(conv_grad),
        on_chip(skip),
        on_chip(query_here),
        on_chip(key_here),
        *back_moved,
    )


def solution(mesh):
    in_specs = (
        P("ctx", "head"),
        P("ctx", "head"),
        P("ctx", "head"),
        P("ctx", "head"),
        P("head", None),
        P("head", None),
        P("head"),
        P(),
        P("head"),
    )
    out_specs = (P("ctx", "head"), P("ctx", "head"), P("head", "ctx"))

    def body(*args):
        return tuple(per_device(*args))

    return jax.shard_map(body, mesh=mesh, in_specs=in_specs, out_specs=out_specs, check_vma=False)
```

```python
import functools

import jax
import jax.numpy as jnp
from jax import lax
from jax.experimental import pallas as pl
from jax.experimental.pallas import tpu as pltpu
from jax.sharding import PartitionSpec as P

F32 = jnp.float32
BF16 = jnp.bfloat16
I32 = jnp.int32
NT = (((1,), (1,)), ((), ()))
NN = (((1,), (0,)), ((), ()))
LANES = 128
SWAPS = 2
EXTRA = 8
VMEM = pl.BlockSpec(memory_space=pltpu.VMEM)
SMEM = pl.BlockSpec(memory_space=pltpu.SMEM)
ANY = pl.BlockSpec(memory_space=pl.ANY)


def dot(a, b, dims):
    return lax.dot_general(a, b, dims, preferred_element_type=F32)


def on_chip(x):
    return pltpu.with_memory_space_constraint(x, pltpu.VMEM)


def call(kernel, out_shape, in_specs, scratch=(), out_specs=None):
    return pl.pallas_call(
        kernel,
        out_shape=out_shape,
        in_specs=in_specs,
        out_specs=jax.tree.map(lambda _: VMEM, out_shape) if out_specs is None else out_specs,
        scratch_shapes=scratch,
        compiler_params=pltpu.CompilerParams(vmem_limit_bytes=56 * 1024 * 1024),
    )


def rank_column(rank_row, column_ref):
    wide = jnp.broadcast_to(rank_row.astype(F32), (LANES, rank_row.shape[1]))
    column_ref[...] = wide.T.astype(I32)


def permute(by_token, column_ref, starts, width, store):
    channels = column_ref.shape[0]
    lane = lax.broadcasted_iota(I32, (channels, LANES), 1)
    unit = min(width, LANES)
    per_dot = max(1, 2 * LANES // width)
    for i in range(0, len(starts), per_dot):
        picks = []
        for start in starts[i : i + per_dot]:
            for q in range(0, width, unit):
                picks.append((start + q, unit))
        mats = []
        per_tile = LANES // unit
        for j in range(0, len(picks), per_tile):
            want = lane + picks[j][0]
            for t in range(1, per_tile):
                want = jnp.where(lane >= t * unit, lane + (picks[j + t][0] - t * unit), want)
            mats.append(jnp.where(column_ref[...] == want, 1.0, 0.0).astype(BF16))
        moved = dot(by_token, jnp.concatenate(mats, axis=1), NN).T.astype(BF16)
        for j in range(min(per_dot, len(starts) - i)):
            store(i + j, moved[j * width : (j + 1) * width])


def split_pair(ctx, full_ref, mine_ref, other_ref):
    place = ctx & 1
    pair = ctx >> 1
    for p in range(mine_ref.shape[0]):
        mine_ref[pair ^ p] = full_ref[2 * p + place]
        other_ref[pair ^ p] = full_ref[2 * p + 1 - place]


def distances(count):
    ring = count // 4

    def hops(e):
        return (e & 1) + min(e >> 1, ring - (e >> 1))

    return [0] + sorted(range(1, count // 2), key=lambda e: (-hops(e), -(e == 4), e))


def join_pair(ctx, packs, full_ref):
    for e, pack in zip(distances(2 * len(packs)), packs):
        full_ref[ctx ^ (2 * e)] = pack[0]
        full_ref[ctx ^ (2 * e + 1)] = pack[1]


def pack_kernel(mine_ref, got_ref, *packs):
    for e, pack in zip(distances(2 * len(packs)), packs):
        pack[0] = mine_ref[e]
        pack[1] = got_ref[e]


def exchange(mine, swap_other, count):
    got = lax.ppermute(on_chip(swap_other), "ctx", [(i, i ^ 1) for i in range(count)])
    mine = mine()
    shape = pltpu.VMEM((2,) + mine.shape[1:], BF16)
    packs = call(pack_kernel, (shape,) * (count // 2), [VMEM, VMEM])(
        on_chip(mine), on_chip(got)
    )
    out = []
    for e, pack in zip(distances(count), packs):
        moved = lax.ppermute(on_chip(pack), "ctx", [(i, i ^ (2 * e)) for i in range(count)]) if e else pack
        out.append(on_chip(moved))
    return out


def stream_weights(first, weight_hbm, weight_ref, sem):
    count = sem.shape[0]
    width = weight_ref.shape[1] // count
    return [
        pltpu.make_async_copy(
            weight_hbm.at[:, pl.ds(pl.multiple_of(first + j * width, LANES), width)],
            weight_ref.at[:, pl.ds(j * width, width)],
            sem.at[j],
        )
        for j in range(count)
    ]


def product(copies, grad_ref, weight_ref, out_ref, fresh):
    width = weight_ref.shape[1] // len(copies)
    for j, copy in enumerate(copies):
        copy.wait()
        cols = slice(j * width, (j + 1) * width)
        part = dot(grad_ref[:, cols], weight_ref[:, cols], NT)
        out_ref[...] = part if fresh and j == 0 else out_ref[...] + part


def begin_kernel(
    first_ref, group_hbm, query_hbm, key_hbm, grad_hbm, weight_hbm, out_hbm, rank_ref, acc_ref,
    group_ref, query_ref, key_ref, grad_ref, weight_ref, out_ref, column_ref, sem, weight_sem, store_sem, *, groups, per_group
):
    loads = [
        pltpu.make_async_copy(group_hbm, group_ref, sem.at[0]),
        pltpu.make_async_copy(query_hbm, query_ref, sem.at[1]),
        pltpu.make_async_copy(key_hbm, key_ref, sem.at[2]),
        pltpu.make_async_copy(grad_hbm, grad_ref, sem.at[3]),
    ]
    for load in loads:
        load.start()
    channels = group_ref.shape[1]
    upper = lax.broadcasted_iota(I32, (LANES, LANES), 0) < lax.broadcasted_iota(I32, (LANES, LANES), 1)
    upper = jnp.where(upper, 1.0, 0.0).astype(BF16)
    base = jnp.zeros((groups, 1), F32)
    loads[0].wait()
    local = group_ref[...] & (groups - 1)
    for b in range(channels // LANES):
        here = local[:, b * LANES : (b + 1) * LANES]
        member = jnp.where(lax.broadcasted_iota(I32, (groups, LANES), 0) == here, 1.0, 0.0)
        before = dot(member.astype(BF16), upper, NN) + base
        place = jnp.sum(member * before, axis=0, keepdims=True)
        rank_ref[:, b * LANES : (b + 1) * LANES] = here * per_group + place.astype(I32)
        base = base + jnp.sum(member, axis=1, keepdims=True)
    rank_column(rank_ref[...], column_ref)
    for load in loads[1:]:
        load.wait()
    copies = stream_weights(first_ref[0], weight_hbm, weight_ref, weight_sem)
    for copy in copies:
        copy.start()
    gated = (query_ref[...].astype(F32) * key_ref[...].astype(F32)).astype(BF16)
    rows = out_ref.shape[1]

    def save(i, block):
        out_ref[i] = block

    permute(gated, column_ref, range(0, channels, rows), rows, save)
    store = pltpu.make_async_copy(out_ref, out_hbm, store_sem)
    store.start()
    product(copies, grad_ref, weight_ref, acc_ref, True)
    store.wait()


def more_kernel(first_ref, grad_ref, acc_ref, weight_hbm, out_ref, weight_ref, sem):
    copies = stream_weights(first_ref[0], weight_hbm, weight_ref, sem)
    for copy in copies:
        copy.start()
    out_ref[...] = acc_ref[...]
    product(copies, grad_ref, weight_ref, out_ref, False)


def pair_blocks(ctx, place, by_token, column_ref, out_ref):
    pairs, rows, _ = out_ref.shape

    def store(p, block):
        out_ref[(ctx >> 1) ^ p] = block

    permute(by_token, column_ref, [(2 * p + place) * rows for p in range(pairs)], rows, store)


def last_kernel(
    first_ref, ctx_ref, rank_ref, grad_ref, acc_ref, weight_hbm, value_hbm, out_ref, conv_ref, total_ref, weight_ref, value_ref, column_ref, sem, value_sem
):
    load = pltpu.make_async_copy(value_hbm, value_ref, value_sem)
    copies = stream_weights(first_ref[0], weight_hbm, weight_ref, sem)
    for copy in copies:
        copy.start()
    load.start()
    rank_column(rank_ref[...], column_ref)
    total_ref[...] = acc_ref[...]
    product(copies, grad_ref, weight_ref, total_ref, False)
    load.wait()
    conv_ref[...] = (total_ref[...] * value_ref[...].astype(F32)).astype(BF16)
    ctx = ctx_ref[0]
    pair_blocks(ctx, 1 - (ctx & 1), conv_ref[...], column_ref, out_ref)


def mine_kernel(ctx_ref, rank_ref, conv_ref, out_ref, column_ref):
    rank_column(rank_ref[...], column_ref)
    ctx = ctx_ref[0]
    pair_blocks(ctx, ctx & 1, conv_ref[...], column_ref, out_ref)


def prepare_kernel(docs_ref, filt_ref, gate_ref, skip_ref, gate_t_ref, rows_ref, doc_ref, skip_out_ref, *, per_group):
    spans, _, tokens = gate_ref.shape
    groups, lags = filt_ref.shape
    flip = lax.broadcasted_iota(I32, (tokens, tokens), 0) + lax.broadcasted_iota(I32, (tokens, tokens), 1)
    flip = jnp.where(flip == tokens - 1, 1.0, 0.0).astype(BF16)
    for g in range(groups):
        gate = gate_ref[:, g * per_group : (g + 1) * per_group, :].reshape(spans * per_group, tokens)
        gate_t_ref[g] = dot(flip, gate, NT).astype(BF16)
    rows_ref[:, :lags] = filt_ref[...]
    rows_ref[:, lags:] = jnp.zeros((groups, tokens), F32)
    index = lax.broadcasted_iota(I32, doc_ref.shape, 0) // per_group
    bound = 0
    doc = jnp.zeros(doc_ref.shape, F32)
    for d in range(docs_ref.shape[0]):
        bound = bound + docs_ref[d]
        doc = doc + jnp.where(index >= bound, 1.0, 0.0)
    doc_ref[...] = doc
    skip_out_ref[...] = skip_ref[...]


def conv_kernel(ctx_ref, gate_t_ref, rows_ref, doc_ref, *refs, per_group):
    *packs, mine_ref, other_ref, grad_ref, out_ref, moved_ref, sums_ref = refs
    join_pair(ctx_ref[0], packs, grad_ref)
    spans, sub, tokens = grad_ref.shape
    groups, padded = rows_ref.shape
    lags = padded - tokens
    reach = lags // tokens
    for k in range(reach):
        cut = k * per_group
        keep = (spans - k) * per_group
        same = jnp.where(doc_ref[cut:, :] == doc_ref[:keep, :], 1.0, 0.0).astype(BF16)
        cols = slice(k * tokens, (k + 1) * tokens)
        for g in range(groups):
            grad = grad_ref[k:, g * per_group : (g + 1) * per_group, :].reshape(keep, tokens)
            moved_ref[g, :keep, cols] = grad * same
            if k:
                moved_ref[g, keep:, cols] = jnp.zeros((cut, tokens), BF16)
    sums_ref[...] = jnp.zeros(sums_ref.shape, F32)
    for g in range(groups):
        moved = moved_ref[g]
        wide = jnp.broadcast_to(rows_ref[g : g + 1, :], (tokens, padded))
        toeplitz = pltpu.roll(wide, 0, 1, stride=1, stride_axis=0)[:, :lags].astype(BF16)
        back = dot(moved, toeplitz, NT)
        out_ref[:, g * per_group : (g + 1) * per_group, :] = back.astype(BF16).reshape(spans, per_group, tokens)
        corr = dot(gate_t_ref[g], moved, NN)
        wide = jnp.concatenate([corr, jnp.zeros((tokens, tokens), F32)], axis=1)
        skewed = pltpu.roll(wide, lags + 1, 1, stride=1, stride_axis=0)
        sums_ref[g : g + 1, :] = jnp.sum(skewed[:, :lags], axis=0, keepdims=True)
    for k in range(spans):
        if k < reach:
            out_ref[k, sub:, :] = sums_ref[:, k * tokens : (k + 1) * tokens].astype(BF16)
        else:
            out_ref[k, sub:, :] = jnp.zeros((EXTRA, tokens), BF16)
    split_pair(ctx_ref[0], out_ref, mine_ref, other_ref)


def fetch_kernel(query_hbm, key_hbm, query_ref, key_ref, sem):
    loads = [
        pltpu.make_async_copy(query_hbm, query_ref, sem.at[0]),
        pltpu.make_async_copy(key_hbm, key_ref, sem.at[1]),
    ]
    for load in loads:
        load.start()
    for load in loads:
        load.wait()


def gates_kernel(
    ctx_ref, rank_ref, conv_ref, skip_ref, query_ref, key_ref, *refs, sub_groups
):
    *packs, grad_query_hbm, grad_key_hbm, filt_hbm = refs[:-7]
    grad_query_ref, grad_key_ref, filt_ref, sorted_ref, back_ref, store_sem, filt_sem = refs[-7:]
    join_pair(ctx_ref[0], packs, back_ref)
    spans, rows, tokens = back_ref.shape
    sub = rows - EXTRA
    channels = rank_ref.shape[1]
    sorted_ref[...] = back_ref[:, :sub, :].reshape(spans * sub, tokens).T
    for d in range(spans):
        filt_ref[d * sub_groups : (d + 1) * sub_groups, :] = back_ref[d, sub:, :].astype(F32)[:sub_groups]
    stores = [pltpu.make_async_copy(filt_ref, filt_hbm, filt_sem)]
    stores[0].start()
    width = channels // store_sem.shape[1]
    for j in range(store_sem.shape[1]):
        cols = slice(j * width, (j + 1) * width)
        place = lax.broadcasted_iota(I32, (channels, width), 0)
        picks = jnp.where(place == rank_ref[:, cols], 1.0, 0.0).astype(BF16)
        gated_grad = dot(sorted_ref[...], picks, NN) + conv_ref[:, cols].astype(F32) * skip_ref[:, cols]
        grad_query_ref[:, cols] = (gated_grad * key_ref[:, cols].astype(F32)).astype(BF16)
        grad_key_ref[:, cols] = (gated_grad * query_ref[:, cols].astype(F32)).astype(BF16)
        for which, (source, target) in enumerate(((grad_query_ref, grad_query_hbm), (grad_key_ref, grad_key_hbm))):
            part = pl.ds(j * width, width)
            stores.append(pltpu.make_async_copy(source.at[:, part], target.at[:, part], store_sem.at[which, j]))
            stores[-1].start()
    for store in stores:
        store.wait()


def per_device(
    query_proj, key_proj, value_proj, grad_out, out_proj, filters, skip_gain, doc_lengths, group_of
):
    tokens, channels = query_proj.shape
    groups = filters.shape[0]
    per_group = channels // groups
    spans = lax.axis_size("ctx")
    heads = lax.axis_size("head")
    position = lax.axis_index("ctx")
    ctx = position.reshape(1)
    head = lax.axis_index("head")
    sub = channels // spans
    sub_groups = sub // per_group
    lags = (spans // 2 + 1) * tokens
    dma = pltpu.SemaphoreType.DMA
    wide = pltpu.VMEM((tokens, channels), BF16)
    column = pltpu.VMEM((channels, LANES), I32)

    feats = grad_out.shape[1]
    width = feats // SWAPS
    arrived = []
    for r in range(1, heads):
        for q in range(SWAPS):
            piece = grad_out[:, q * width : (q + 1) * width]
            moved = lax.ppermute(piece, "head", [(i, (i + r) % heads) for i in range(heads)])
            arrived.append((((head + heads - r) % heads) * feats + q * width, moved))

    def weights(size):
        return [pltpu.VMEM((channels, size), BF16)], dma((max(1, size // (2 * LANES)),))

    scratch, sems = weights(feats)
    gate_sorted, rank, acc = call(
        functools.partial(begin_kernel, groups=groups, per_group=per_group),
        (
            jax.ShapeDtypeStruct((spans, sub, tokens), BF16),
            pltpu.VMEM((1, channels), I32),
            pltpu.VMEM((tokens, channels), F32),
        ),
        [SMEM, ANY, ANY, ANY, ANY, ANY],
        [pltpu.VMEM((1, channels), I32), wide, wide, pltpu.VMEM((tokens, feats), BF16)]
        + scratch
        + [pltpu.VMEM((spans, sub, tokens), BF16), column, dma((4,)), sems, dma],
        (ANY, VMEM, VMEM),
    )((head * feats).reshape(1), group_of.reshape(1, channels), query_proj, key_proj, grad_out, out_proj)
    rank, acc = on_chip(rank), on_chip(acc)
    gate_moved = lax.all_to_all(gate_sorted, "ctx", 0, 0)

    scratch, sems = weights(width)
    for p, (first, grad) in enumerate(arrived):
        if p < len(arrived) - 1:
            acc = call(
                more_kernel, pltpu.VMEM((tokens, channels), F32), [SMEM, VMEM, VMEM, ANY], scratch + [sems]
            )(first.reshape(1), on_chip(grad), acc, out_proj)
            acc = on_chip(acc)
        else:
            conv_sorted, conv_grad = call(
                last_kernel,
                (pltpu.VMEM((spans // 2, sub, tokens), BF16), pltpu.VMEM((tokens, channels), BF16)),
                [SMEM, SMEM, VMEM, VMEM, VMEM, ANY, ANY],
                [pltpu.VMEM((tokens, channels), F32)] + scratch + [wide, column, sems, dma],
            )(first.reshape(1), ctx, rank, on_chip(grad), acc, out_proj, value_proj)

    def conv_mine():
        return call(
            mine_kernel, pltpu.VMEM((spans // 2, sub, tokens), BF16), [SMEM, VMEM, VMEM], [column]
        )(ctx, on_chip(rank), on_chip(conv_grad))

    conv_moved = exchange(conv_mine, conv_sorted, spans)

    filt_sub = lax.dynamic_slice(filters, (position * sub_groups, 0), (sub_groups, lags)).astype(F32)
    gate_t, rows, doc, skip = call(
        functools.partial(prepare_kernel, per_group=per_group),
        (
            pltpu.VMEM((sub_groups, tokens, spans * per_group), BF16),
            pltpu.VMEM((sub_groups, lags + tokens), F32),
            pltpu.VMEM((spans * per_group, tokens), F32),
            pltpu.VMEM((1, channels), F32),
        ),
        [SMEM, VMEM, VMEM, VMEM],
    )(doc_lengths, filt_sub, on_chip(gate_moved), skip_gain.reshape(1, channels))

    back, back_other = call(
        functools.partial(conv_kernel, per_group=per_group),
        (pltpu.VMEM((spans // 2, sub + EXTRA, tokens), BF16),) * 2,
        [SMEM] + [VMEM] * (3 + spans // 2),
        [
            pltpu.VMEM((spans, sub, tokens), BF16),
            pltpu.VMEM((spans, sub + EXTRA, tokens), BF16),
            pltpu.VMEM((sub_groups, spans * per_group, lags), BF16),
            pltpu.VMEM((EXTRA, lags), F32),
        ],
    )(ctx, on_chip(gate_t), on_chip(rows), on_chip(doc), *conv_moved)
    query_here, key_here = call(fetch_kernel, (wide, wide), [ANY, ANY], [dma((2,))])(query_proj, key_proj)
    back_moved = exchange(lambda: back, back_other, spans)

    return call(
        functools.partial(gates_kernel, sub_groups=sub_groups),
        (
            jax.ShapeDtypeStruct((tokens, channels), BF16),
            jax.ShapeDtypeStruct((tokens, channels), BF16),
            jax.ShapeDtypeStruct((groups, tokens), F32),
        ),
        [SMEM] + [VMEM] * (5 + spans // 2),
        [wide, wide, pltpu.VMEM((groups, tokens), F32), wide]
        + [pltpu.VMEM((spans, sub + EXTRA, tokens), BF16), dma((2, min(8, channels // LANES))), dma],
        (ANY, ANY, ANY),
    )(
        ctx,
        on_chip(rank),
        on_chip(conv_grad),
        on_chip(skip),
        on_chip(query_here),
        on_chip(key_here),
        *back_moved,
    )


def solution(mesh):
    in_specs = (
        P("ctx", "head"),
        P("ctx", "head"),
        P("ctx", "head"),
        P("ctx", "head"),
        P("head", None),
        P("head", None),
        P("head"),
        P(),
        P("head"),
    )
    out_specs = (P("ctx", "head"), P("ctx", "head"), P("head", "ctx"))

    def body(*args):
        return tuple(per_device(*args))

    return jax.shard_map(body, mesh=mesh, in_specs=in_specs, out_specs=out_specs, check_vma=False)
```

```python
import functools

import jax
import jax.numpy as jnp
from jax import lax
from jax.experimental import pallas as pl
from jax.experimental.pallas import tpu as pltpu
from jax.sharding import PartitionSpec as P

F32 = jnp.float32
BF16 = jnp.bfloat16
I32 = jnp.int32
NT = (((1,), (1,)), ((), ()))
NN = (((1,), (0,)), ((), ()))
LANES = 128
EXTRA = 8
VMEM = pl.BlockSpec(memory_space=pltpu.VMEM)
SMEM = pl.BlockSpec(memory_space=pltpu.SMEM)
ANY = pl.BlockSpec(memory_space=pl.ANY)


def dot(a, b, dims):
    return lax.dot_general(a, b, dims, preferred_element_type=F32)


def on_chip(x):
    return pltpu.with_memory_space_constraint(x, pltpu.VMEM)


def call(kernel, out_shape, in_specs, scratch=(), out_specs=None):
    return pl.pallas_call(
        kernel,
        out_shape=out_shape,
        in_specs=in_specs,
        out_specs=jax.tree.map(lambda _: VMEM, out_shape) if out_specs is None else out_specs,
        scratch_shapes=scratch,
        compiler_params=pltpu.CompilerParams(vmem_limit_bytes=56 * 1024 * 1024),
    )


def rank_column(rank_row, column_ref):
    wide = jnp.broadcast_to(rank_row.astype(F32), (LANES, rank_row.shape[1]))
    column_ref[...] = wide.T.astype(I32)


def permute(by_token, column_ref, starts, width, store):
    channels = column_ref.shape[0]
    lane = lax.broadcasted_iota(I32, (channels, LANES), 1)
    unit = min(width, LANES)
    per_dot = max(1, 2 * LANES // width)
    for i in range(0, len(starts), per_dot):
        picks = []
        for start in starts[i : i + per_dot]:
            for q in range(0, width, unit):
                picks.append((start + q, unit))
        mats = []
        per_tile = LANES // unit
        for j in range(0, len(picks), per_tile):
            want = lane + picks[j][0]
            for t in range(1, per_tile):
                want = jnp.where(lane >= t * unit, lane + (picks[j + t][0] - t * unit), want)
            mats.append(jnp.where(column_ref[...] == want, 1.0, 0.0).astype(BF16))
        moved = dot(by_token, jnp.concatenate(mats, axis=1), NN).T.astype(BF16)
        for j in range(min(per_dot, len(starts) - i)):
            store(i + j, moved[j * width : (j + 1) * width])


def split_pair(ctx, full_ref, mine_ref, other_ref):
    place = ctx & 1
    pair = ctx >> 1
    for p in range(mine_ref.shape[0]):
        mine_ref[pair ^ p] = full_ref[2 * p + place]
        other_ref[pair ^ p] = full_ref[2 * p + 1 - place]


def distances(count):
    ring = count // 4

    def hops(e):
        return (e & 1) + min(e >> 1, ring - (e >> 1))

    return [0] + sorted(range(1, count // 2), key=lambda e: (-hops(e), -(e == 4), e))


def pack_kernel(*refs, parts):
    mine, got, packs = refs[:parts], refs[parts : 2 * parts], refs[2 * parts :]
    for e, pack in zip(distances(2 * len(packs)), packs):
        for which, pieces in enumerate((mine, got)):
            at = 0
            for piece in pieces:
                pack[which, at : at + piece.shape[1]] = piece[e]
                at = at + piece.shape[1]


def swap_pair(blocks, count):
    return on_chip(lax.ppermute(on_chip(blocks), "ctx", [(i, i ^ 1) for i in range(count)]))


def spread(mine, got, count):
    rows = sum(piece.shape[1] for piece in mine)
    shape = pltpu.VMEM((2, rows, mine[0].shape[2]), BF16)
    packs = call(
        functools.partial(pack_kernel, parts=len(mine)), (shape,) * (count // 2), [VMEM] * (2 * len(mine))
    )(*[on_chip(piece) for piece in mine], *got)
    out = []
    for e, pack in zip(distances(count), packs):
        moved = lax.ppermute(on_chip(pack), "ctx", [(i, i ^ (2 * e)) for i in range(count)]) if e else pack
        out.append(on_chip(moved))
    return out


def gate_kernel(
    group_hbm, query_hbm, key_hbm, grad_hbm, out_hbm, rank_ref, grad_ref,
    group_ref, query_ref, key_ref, out_ref, column_ref, sem, store_sem, *, groups, per_group
):
    loads = [
        pltpu.make_async_copy(group_hbm, group_ref, sem.at[0]),
        pltpu.make_async_copy(query_hbm, query_ref, sem.at[1]),
        pltpu.make_async_copy(key_hbm, key_ref, sem.at[2]),
        pltpu.make_async_copy(grad_hbm, grad_ref, sem.at[3]),
    ]
    for load in loads:
        load.start()
    channels = group_ref.shape[1]
    upper = lax.broadcasted_iota(I32, (LANES, LANES), 0) < lax.broadcasted_iota(I32, (LANES, LANES), 1)
    upper = jnp.where(upper, 1.0, 0.0).astype(BF16)
    base = jnp.zeros((groups, 1), F32)
    loads[0].wait()
    local = group_ref[...] & (groups - 1)
    for b in range(channels // LANES):
        here = local[:, b * LANES : (b + 1) * LANES]
        member = jnp.where(lax.broadcasted_iota(I32, (groups, LANES), 0) == here, 1.0, 0.0)
        before = dot(member.astype(BF16), upper, NN) + base
        place = jnp.sum(member * before, axis=0, keepdims=True)
        rank_ref[:, b * LANES : (b + 1) * LANES] = here * per_group + place.astype(I32)
        base = base + jnp.sum(member, axis=1, keepdims=True)
    rank_column(rank_ref[...], column_ref)
    for load in loads[1:3]:
        load.wait()
    gated = (query_ref[...].astype(F32) * key_ref[...].astype(F32)).astype(BF16)
    rows = out_ref.shape[1]
    stores = []

    def save(i, block):
        out_ref[i] = block
        stores.append(pltpu.make_async_copy(out_ref.at[i], out_hbm.at[i], store_sem.at[i]))
        stores[-1].start()

    permute(gated, column_ref, range(0, channels, rows), rows, save)
    for copy in [loads[3]] + stores:
        copy.wait()


def stream_weights(half, weight_hbm, weight_ref, sem):
    _, feats = weight_ref.shape
    count = sem.shape[0]
    width = feats // count
    copies = [
        pltpu.make_async_copy(
            weight_hbm.at[:, pl.ds(pl.multiple_of(half * feats + j * width, width), width)],
            weight_ref.at[:, pl.ds(j * width, width)],
            sem.at[j],
        )
        for j in range(count)
    ]
    for copy in copies:
        copy.start()
    return copies, width


def product(copies, width, grad_ref, weight_ref, out_ref, fresh):
    for j, copy in enumerate(copies):
        copy.wait()
        cols = slice(j * width, (j + 1) * width)
        part = dot(grad_ref[:, cols], weight_ref[:, cols], NT)
        out_ref[...] = part if fresh and j == 0 else out_ref[...] + part


def partial_kernel(half_ref, grad_ref, weight_hbm, *refs):
    *acc, out_ref, weight_ref, sem = refs
    copies, width = stream_weights(half_ref[0], weight_hbm, weight_ref, sem)
    if acc:
        out_ref[...] = acc[0][...]
    product(copies, width, grad_ref, weight_ref, out_ref, not acc)


def pair_blocks(ctx, place, by_token, column_ref, out_ref):
    pairs, rows, _ = out_ref.shape

    def store(p, block):
        out_ref[(ctx >> 1) ^ p] = block

    permute(by_token, column_ref, [(2 * p + place) * rows for p in range(pairs)], rows, store)


def last_kernel(
    half_ref, ctx_ref, rank_ref, grad_ref, acc_ref, weight_hbm, value_hbm, out_ref, conv_ref, total_ref, weight_ref, value_ref, column_ref, sem, value_sem
):
    load = pltpu.make_async_copy(value_hbm, value_ref, value_sem)
    copies, width = stream_weights(half_ref[0], weight_hbm, weight_ref, sem)
    load.start()
    rank_column(rank_ref[...], column_ref)
    total_ref[...] = acc_ref[...]
    product(copies, width, grad_ref, weight_ref, total_ref, False)
    load.wait()
    conv_ref[...] = (total_ref[...] * value_ref[...].astype(F32)).astype(BF16)
    ctx = ctx_ref[0]
    pair_blocks(ctx, 1 - (ctx & 1), conv_ref[...], column_ref, out_ref)


def mine_kernel(ctx_ref, rank_ref, conv_ref, out_ref, column_ref):
    rank_column(rank_ref[...], column_ref)
    ctx = ctx_ref[0]
    pair_blocks(ctx, ctx & 1, conv_ref[...], column_ref, out_ref)


def prepare_kernel(docs_ref, filt_ref, gate_ref, skip_ref, gate_t_ref, rows_ref, doc_ref, skip_out_ref, *, per_group):
    spans, _, tokens = gate_ref.shape
    groups, lags = filt_ref.shape
    flip = lax.broadcasted_iota(I32, (tokens, tokens), 0) + lax.broadcasted_iota(I32, (tokens, tokens), 1)
    flip = jnp.where(flip == tokens - 1, 1.0, 0.0).astype(BF16)
    for g in range(groups):
        gate = gate_ref[:, g * per_group : (g + 1) * per_group, :].reshape(spans * per_group, tokens)
        gate_t_ref[g] = dot(flip, gate, NT).astype(BF16)
    rows_ref[:, :lags] = filt_ref[...]
    rows_ref[:, lags:] = jnp.zeros((groups, tokens), F32)
    index = lax.broadcasted_iota(I32, doc_ref.shape, 0) // per_group
    bound = 0
    doc = jnp.zeros(doc_ref.shape, F32)
    for d in range(docs_ref.shape[0]):
        bound = bound + docs_ref[d]
        doc = doc + jnp.where(index >= bound, 1.0, 0.0)
    doc_ref[...] = doc
    skip_out_ref[...] = skip_ref[...]


def conv_kernel(ctx_ref, gate_t_ref, rows_ref, doc_ref, *refs, per_group, first, final):
    *packs, mine_ref, other_ref, total_ref, grad_ref, out_ref, moved_ref = refs
    earlier = packs.pop() if first else None
    spans, sub, tokens = grad_ref.shape
    groups = sub // per_group
    top = first * per_group
    for e, pack in zip(distances(spans), packs):
        grad_ref[ctx_ref[0] ^ (2 * e)] = pack[0, top : top + sub]
        grad_ref[ctx_ref[0] ^ (2 * e + 1)] = pack[1, top : top + sub]
    padded = rows_ref.shape[1]
    lags = padded - tokens
    reach = lags // tokens
    for k in range(reach):
        cut = k * per_group
        keep = (spans - k) * per_group
        same = jnp.where(doc_ref[cut:, :] == doc_ref[:keep, :], 1.0, 0.0).astype(BF16)
        cols = slice(k * tokens, (k + 1) * tokens)
        for g in range(groups):
            grad = grad_ref[k:, g * per_group : (g + 1) * per_group, :].reshape(keep, tokens)
            moved_ref[g, :keep, cols] = grad * same
            if k:
                moved_ref[g, keep:, cols] = jnp.zeros((cut, tokens), BF16)
    total_ref[...] = earlier[...] if first else jnp.zeros(total_ref.shape, F32)
    for g in range(groups):
        moved = moved_ref[g]
        row = slice(first + g, first + g + 1)
        wide = jnp.broadcast_to(rows_ref[row, :], (tokens, padded))
        toeplitz = pltpu.roll(wide, 0, 1, stride=1, stride_axis=0)[:, :lags].astype(BF16)
        back = dot(moved, toeplitz, NT)
        out_ref[:, g * per_group : (g + 1) * per_group, :] = back.astype(BF16).reshape(spans, per_group, tokens)
        corr = dot(gate_t_ref[first + g], moved, NN)
        wide = jnp.concatenate([corr, jnp.zeros((tokens, tokens), F32)], axis=1)
        skewed = pltpu.roll(wide, lags + 1, 1, stride=1, stride_axis=0)
        total_ref[row, :] = jnp.sum(skewed[:, :lags], axis=0, keepdims=True)
    if final:
        for k in range(spans):
            if k < reach:
                out_ref[k, sub:, :] = total_ref[:, k * tokens : (k + 1) * tokens].astype(BF16)
            else:
                out_ref[k, sub:, :] = jnp.zeros((EXTRA, tokens), BF16)
    split_pair(ctx_ref[0], out_ref, mine_ref, other_ref)


def fetch_kernel(query_hbm, key_hbm, after_ref, query_ref, key_ref, sem):
    loads = [
        pltpu.make_async_copy(query_hbm, query_ref, sem.at[0]),
        pltpu.make_async_copy(key_hbm, key_ref, sem.at[1]),
    ]
    for load in loads:
        load.start()
    for load in loads:
        load.wait()


def by_token(packs, sorted_ref):
    sub = packs[0].shape[1] - EXTRA
    for i, pack in enumerate(packs):
        flat = pack[:, :sub, :].reshape(2 * sub, pack.shape[2])
        sorted_ref[:, i * 2 * sub : (i + 1) * 2 * sub] = flat.T


def picks_of(ctx, rank, apart, sub):
    shape = (sub, rank.shape[1])
    row = lax.broadcasted_iota(I32, shape, 0)
    blocks = []
    for e in apart:
        for which in range(2):
            source = ctx ^ (2 * e + which)
            blocks.append(jnp.where(row == rank - source * sub, 1.0, 0.0).astype(BF16))
    return jnp.concatenate(blocks, axis=0)


def restore_kernel(ctx_ref, rank_ref, conv_ref, skip_ref, *refs, apart):
    *packs, out_ref, sorted_ref = refs
    sub = packs[0].shape[1] - EXTRA
    by_token(packs, sorted_ref)
    channels = rank_ref.shape[1]
    width = min(2 * LANES, channels)
    for j in range(0, channels, width):
        cols = slice(j, j + width)
        picks = picks_of(ctx_ref[0], rank_ref[:, cols], apart, sub)
        out_ref[:, cols] = dot(sorted_ref[...], picks, NN) + conv_ref[:, cols].astype(F32) * skip_ref[:, cols]


def gates_kernel(ctx_ref, rank_ref, acc_ref, query_ref, key_ref, *refs, early, sub_groups):
    *packs, grad_query_hbm, grad_key_hbm, filt_hbm = refs[:-6]
    grad_query_ref, grad_key_ref, filt_ref, sorted_ref, store_sem, filt_sem = refs[-6:]
    channels = rank_ref.shape[1]
    sub = packs[0].shape[1] - EXTRA
    apart = distances(2 * len(packs))
    by_token(packs[early:], sorted_ref)
    for e, pack in zip(apart, packs):
        for which in range(2):
            filt_ref[ctx_ref[0] ^ (2 * e + which)] = pack[which, sub:, :].astype(F32)[:sub_groups]
    stores = [pltpu.make_async_copy(filt_ref, filt_hbm, filt_sem)]
    stores[0].start()
    width = channels // store_sem.shape[1]
    for j in range(store_sem.shape[1]):
        cols = slice(j * width, (j + 1) * width)
        picks = picks_of(ctx_ref[0], rank_ref[:, cols], apart[early:], sub)
        gated_grad = acc_ref[:, cols] + dot(sorted_ref[...], picks, NN)
        grad_query_ref[:, cols] = (gated_grad * key_ref[:, cols].astype(F32)).astype(BF16)
        grad_key_ref[:, cols] = (gated_grad * query_ref[:, cols].astype(F32)).astype(BF16)
        for which, (source, target) in enumerate(((grad_query_ref, grad_query_hbm), (grad_key_ref, grad_key_hbm))):
            part = pl.ds(j * width, width)
            stores.append(pltpu.make_async_copy(source.at[:, part], target.at[:, part], store_sem.at[which, j]))
            stores[-1].start()
    for store in stores:
        store.wait()


def per_device(
    query_proj, key_proj, value_proj, grad_out, out_proj, filters, skip_gain, doc_lengths, group_of
):
    tokens, channels = query_proj.shape
    groups = filters.shape[0]
    per_group = channels // groups
    spans = lax.axis_size("ctx")
    heads = lax.axis_size("head")
    position = lax.axis_index("ctx")
    ctx = position.reshape(1)
    head = lax.axis_index("head")
    sub = channels // spans
    sub_groups = sub // per_group
    lags = (spans // 2 + 1) * tokens
    feats = grad_out.shape[1]
    dma = pltpu.SemaphoreType.DMA
    wide = pltpu.VMEM((tokens, channels), BF16)
    column = pltpu.VMEM((channels, LANES), I32)

    arrived = [lax.ppermute(grad_out, "head", [(i, (i + r) % heads) for i in range(heads)]) for r in range(1, heads)]

    gate_sorted, rank, grad_here = call(
        functools.partial(gate_kernel, groups=groups, per_group=per_group),
        (
            jax.ShapeDtypeStruct((spans, sub, tokens), BF16),
            pltpu.VMEM((1, channels), I32),
            pltpu.VMEM((tokens, feats), BF16),
        ),
        [ANY, ANY, ANY, ANY],
        [pltpu.VMEM((1, channels), I32), wide, wide, pltpu.VMEM((spans, sub, tokens), BF16)]
        + [column, dma((4,)), dma((spans,))],
        (ANY, VMEM, VMEM),
    )(group_of.reshape(1, channels), query_proj, key_proj, grad_out)
    gate_moved = lax.all_to_all(gate_sorted, "ctx", 0, 0)

    parts = min(8, feats // LANES)
    acc = None
    for r, grad in enumerate([grad_here] + arrived):
        source = ((head + heads - r) % heads).reshape(1)
        if r < heads - 1:
            acc = call(
                partial_kernel,
                pltpu.VMEM((tokens, channels), F32),
                [SMEM, VMEM, ANY] + ([] if acc is None else [VMEM]),
                [pltpu.VMEM((channels, feats), BF16), dma((parts,))],
            )(source, on_chip(grad), out_proj, *([] if acc is None else [acc]))
            acc = on_chip(acc)
        else:
            conv_sorted, conv_grad = call(
                last_kernel,
                (pltpu.VMEM((spans // 2, sub, tokens), BF16), pltpu.VMEM((tokens, channels), BF16)),
                [SMEM, SMEM, VMEM, VMEM, VMEM, ANY, ANY],
                [
                    pltpu.VMEM((tokens, channels), F32),
                    pltpu.VMEM((channels, feats), BF16),
                    wide,
                    column,
                    dma((parts,)),
                    dma,
                ],
            )(source, ctx, on_chip(rank), on_chip(grad), acc, out_proj, value_proj)
    got = swap_pair(conv_sorted, spans)
    mine = call(
        mine_kernel, pltpu.VMEM((spans // 2, sub, tokens), BF16), [SMEM, VMEM, VMEM], [column]
    )(ctx, on_chip(rank), on_chip(conv_grad))
    conv_moved = spread([mine], [got], spans)

    filt_sub = lax.dynamic_slice(filters, (position * sub_groups, 0), (sub_groups, lags)).astype(F32)
    gate_t, rows, doc, skip = call(
        functools.partial(prepare_kernel, per_group=per_group),
        (
            pltpu.VMEM((sub_groups, tokens, spans * per_group), BF16),
            pltpu.VMEM((sub_groups, lags + tokens), F32),
            pltpu.VMEM((spans * per_group, tokens), F32),
            pltpu.VMEM((1, channels), F32),
        ),
        [SMEM, VMEM, VMEM, VMEM],
    )(doc_lengths, filt_sub, on_chip(gate_moved), skip_gain.reshape(1, channels))

    mine, got, sums = [], [], []
    tail = max(1, sub_groups // 4)
    for first, count in ((0, sub_groups - tail), (sub_groups - tail, tail)):
        final = first > 0
        part = count * per_group
        full = part + (EXTRA if final else 0)
        back, other, total = call(
            functools.partial(conv_kernel, per_group=per_group, first=first, final=final),
            (pltpu.VMEM((spans // 2, full, tokens), BF16),) * 2 + (pltpu.VMEM((EXTRA, lags), F32),),
            [SMEM] + [VMEM] * (3 + spans // 2 + len(sums)),
            [
                pltpu.VMEM((spans, part, tokens), BF16),
                pltpu.VMEM((spans, full, tokens), BF16),
                pltpu.VMEM((count, spans * per_group, lags), BF16),
            ],
        )(ctx, on_chip(gate_t), on_chip(rows), on_chip(doc), *conv_moved, *sums)
        sums = [on_chip(total)]
        mine.append(back)
        got.append(swap_pair(other, spans))
    back_moved = spread(mine, got, spans)

    early = 3
    apart = distances(spans)
    acc = on_chip(
        call(
            functools.partial(restore_kernel, apart=apart[:early]),
            pltpu.VMEM((tokens, channels), F32),
            [SMEM] + [VMEM] * (3 + early),
            [pltpu.VMEM((tokens, early * 2 * sub), BF16)],
        )(ctx, on_chip(rank), on_chip(conv_grad), on_chip(skip), *back_moved[:early])
    )
    query_here, key_here = call(fetch_kernel, (wide, wide), [ANY, ANY, VMEM], [dma((2,))])(query_proj, key_proj, acc)
    grad_query, grad_key, grad_filters = call(
        functools.partial(gates_kernel, early=early, sub_groups=sub_groups),
        (
            jax.ShapeDtypeStruct((tokens, channels), BF16),
            jax.ShapeDtypeStruct((tokens, channels), BF16),
            jax.ShapeDtypeStruct((spans, sub_groups, tokens), F32),
        ),
        [SMEM] + [VMEM] * (4 + spans // 2),
        [wide, wide, pltpu.VMEM((spans, sub_groups, tokens), F32)]
        + [pltpu.VMEM((tokens, channels - early * 2 * sub), BF16)]
        + [dma((2, min(8, channels // LANES))), dma],
        (ANY, ANY, ANY),
    )(ctx, on_chip(rank), acc, on_chip(query_here), on_chip(key_here), *back_moved)
    return grad_query, grad_key, grad_filters.reshape(groups, tokens)


def solution(mesh):
    in_specs = (
        P("ctx", "head"),
        P("ctx", "head"),
        P("ctx", "head"),
        P("ctx", "head"),
        P("head", None),
        P("head", None),
        P("head"),
        P(),
        P("head"),
    )
    out_specs = (P("ctx", "head"), P("ctx", "head"), P("head", "ctx"))

    def body(*args):
        return tuple(per_device(*args))

    return jax.shard_map(body, mesh=mesh, in_specs=in_specs, out_specs=out_specs, check_vma=False)
```
